32 devices in a mesh: ctx: 8 (over y, x, core), head: 4 (over z).
Axes of the slice: x: 2, y: 2, z: 4, core: 2. Of those that a mesh axis runs over, the one named last changes fastest.
Arguments:
- queries: bfloat16 [4096, 4096], P(('ctx', 'head')), may hold values from -128 to 128
- vis_feats: bfloat16 [4096, 8192], P('ctx', 'head'), may hold values from -16 to 16
- kv_weight: bfloat16 [8192, 1024], P('head'), may hold values from -0.044194174 to 0.044194174
- key_gain: float32 [128], replicated, may hold values from 0.1 to 1.9
- cross_mask: int32 [4096, 4], P('ctx'), may hold values 0 or 1
- image_tokens: int32 [4], replicated, may hold values from 1 to 512, 1280 in all
- image_owner: int32 [4], replicated, may hold values from 0 to 7, as said below
Outputs:
- attended: bfloat16 [4096, 4096], P(('ctx', 'head'))
The draws below stay inside these ranges and needn't reach their ends.
Inputs may be any that keep to these rules, and one draw needn't show every extreme that they name: `image_tokens`: they sum to 1280; the largest is exactly 512. `image_owner`: four distinct context indices; the first and the last index of ctx always hold an image.
All inputs are finite; a program needn't handle non-finite values. No bound on the sum of `cross_mask` on one device may be relied on, other than what follows from the above.
Results may differ from the reference program's by a relative error of at most 0.0014.
The reference program's roundings to bfloat16 on the way count: a program that leaves them out, or rounds other values in their place, can miss the bound.
Values may be sent and summed in bfloat16 or wider, within the bound.
No kernel may reach another device: no remote copies, remote signals or barrier semaphores. Data moves between devices by JAX's collectives and lax.ppermute only.
A program may use at most 64 MiB of HBM per device.

```python
import math
import jax
import jax.numpy as jnp
import numpy as np
from jax import lax

MODEL_WIDTH = 8192
HEAD_SIZE = 128
QUERY_HEAD_COUNT = 32
KEY_VALUE_HEADS = 4
NIMG = 4
IMAGE_TOKEN_MAX = 512
KV_TOTAL = 1280
TOKENS = 4096
N_CTX = 8


def shared_parts(key):
    weight_matrix = jnp.clip(jax.random.normal(jax.random.fold_in(key, 12), (MODEL_WIDTH, 2 * KEY_VALUE_HEADS * HEAD_SIZE), jnp.float32), -4.0, 4.0) * MODEL_WIDTH ** (-0.5)
    return weight_matrix


def draw_kv_weight(key, part):
    return shared_parts(key).astype(jnp.bfloat16)


def draw_vis_feats(key, part):
    noise = jnp.clip(jax.random.normal(jax.random.fold_in(key, 13), (N_CTX * IMAGE_TOKEN_MAX, MODEL_WIDTH), jnp.float32), -4.0, 4.0)
    return noise.astype(jnp.bfloat16)


def draw_queries(key, part):
    drawn = jnp.clip(jax.random.normal(jax.random.fold_in(key, 14), (TOKENS, QUERY_HEAD_COUNT * HEAD_SIZE), jnp.float32), -4.0, 4.0)
    return drawn.astype(jnp.bfloat16)


def draw_image_owner(key, part):
    middle = jax.random.permutation(jax.random.fold_in(key, 21), N_CTX - 2)[:2] + 1
    chosen = jnp.concatenate([jnp.array([0, N_CTX - 1], dtype=jnp.int32), middle.astype(jnp.int32)])
    return jax.random.permutation(jax.random.fold_in(key, 22), chosen).astype(jnp.int32)


def set_ends(values, own_key, least, high):
    longest = values.shape.index(max(values.shape))
    spots = []
    for shift in (0, 1):
        where = [jax.random.randint(jax.random.fold_in(own_key, axis), (), 0, length) for axis, length in enumerate(values.shape)]
        where[longest] = (where[longest] + shift) % values.shape[longest]
        spots.append(tuple(where))
    return values.at[spots[0]].set(least).at[spots[1]].set(high)


def split_up(count, total, most, skew):
    loads = [(1 << 20) // math.isqrt(rank ** skew) + 1 for rank in range(2, count + 1)]
    rest, given = total - most - (count - 1), [1] * (count - 1)
    while rest > 0:
        free = [i for i in range(count - 1) if given[i] < most]
        whole, budget = sum([loads[i] for i in free]), rest
        for i in free:
            addition = min(most - given[i], max(1, budget * loads[i] // whole), rest)
            given[i] = given[i] + addition
            rest = rest - addition
    return np.array([most] + given)


def uneven_parts(stream_key, count, total, bound, skew):
    if count == 2:
        one = jax.random.randint(stream_key, (), max(1, total - bound), min(bound, total - 1) + 1)
        return jnp.stack([one, total - one])
    sizes = jnp.asarray(split_up(count, total, bound, skew), jnp.int32)
    pairs = (count - 1) // 2
    source_of, sink = sizes[1:1 + 2 * pairs:2], sizes[2:2 + 2 * pairs:2]
    slack = jnp.minimum(source_of - 1, bound - sink)
    moved = jax.random.randint(jax.random.fold_in(stream_key, 1), (pairs,), 0, 1 << 20) % (slack + 1)
    sizes = sizes.at[1:1 + 2 * pairs:2].set(source_of - moved).at[2:2 + 2 * pairs:2].set(sink + moved)
    return sizes[jax.random.permutation(jax.random.fold_in(stream_key, 2), count)]


def setup_inputs(seed: int = 0) -> dict:
    arg_keys = jax.random.split(jax.random.key(seed), 8)
    queries = draw_queries(jax.random.fold_in(arg_keys[7], 71), 0)
    vis_feats = draw_vis_feats(jax.random.fold_in(arg_keys[7], 71), 0)
    kv_weight = draw_kv_weight(jax.random.fold_in(arg_keys[7], 71), 0)
    key_gain = jnp.clip(1.0 + 0.18 * jax.random.normal(arg_keys[3], (HEAD_SIZE,), jnp.float32), 0.1, 1.9)
    cross_mask = set_ends((jax.random.randint(arg_keys[4], (TOKENS, NIMG), 0, 4) < 3).astype(jnp.int32), jax.random.fold_in(arg_keys[4], 1), 0, 1)
    image_tokens = uneven_parts(arg_keys[5], NIMG, KV_TOTAL, IMAGE_TOKEN_MAX, 2).astype(jnp.int32)
    image_owner = draw_image_owner(jax.random.fold_in(arg_keys[7], 71), 0)
    return {"queries": queries, "vis_feats": vis_feats, "kv_weight": kv_weight, "key_gain": key_gain, "cross_mask": cross_mask, "image_tokens": image_tokens, "image_owner": image_owner}


EPSILON = 1e-05

def project_image(vis_feats, kv_weight, key_gain, owner_idx):
    first_row = (owner_idx * IMAGE_TOKEN_MAX).astype(jnp.int32)
    rows_img = lax.dynamic_slice_in_dim(vis_feats, first_row, IMAGE_TOKEN_MAX, 0)
    projected_rows = jnp.dot(rows_img, kv_weight, preferred_element_type=jnp.float32)
    projected_rows = projected_rows.reshape(IMAGE_TOKEN_MAX, KEY_VALUE_HEADS, 2, HEAD_SIZE)
    raw_keys = projected_rows[:, :, 0, :]
    square_mean = lax.optimization_barrier(jnp.mean(raw_keys * raw_keys, axis=-1, keepdims=True))
    normed = raw_keys * lax.rsqrt(square_mean + EPSILON) * key_gain
    return (normed.astype(jnp.bfloat16), projected_rows[:, :, 1, :].astype(jnp.bfloat16))

def reference(queries, vis_feats, kv_weight, key_gain, cross_mask, image_tokens, image_owner):
    key_parts = []
    value_parts = []
    for img_index in range(NIMG):
        normed, values = project_image(vis_feats, kv_weight, key_gain, image_owner[img_index])
        key_parts.append(normed)
        value_parts.append(values)
    key_all = lax.optimization_barrier(jnp.concatenate(key_parts, 0)).astype(jnp.float32)
    value_all = lax.optimization_barrier(jnp.concatenate(value_parts, 0)).astype(jnp.float32)
    positions = jnp.arange(NIMG * IMAGE_TOKEN_MAX, dtype=jnp.int32)
    key_image = positions // IMAGE_TOKEN_MAX
    key_slot = positions % IMAGE_TOKEN_MAX
    key_valid = key_slot < image_tokens[key_image]
    onehot = ((key_image[:, None] == jnp.arange(NIMG, dtype=jnp.int32)[None, :]) & key_valid[:, None]).astype(jnp.float32)
    rows_per_block = min(1024, TOKENS)
    count_of_blocks = TOKENS // rows_per_block
    blocked_queries = queries.reshape(count_of_blocks, rows_per_block, KEY_VALUE_HEADS, QUERY_HEAD_COUNT // KEY_VALUE_HEADS, HEAD_SIZE)
    mask_blocks = cross_mask.reshape(count_of_blocks, rows_per_block, NIMG)
    factor = HEAD_SIZE ** (-0.5)

    def one_block(block_pair):
        query_block, mask_block = block_pair
        allowed = jnp.dot(mask_block.astype(jnp.float32), onehot.T) > 0.5
        allowed = allowed[:, None, None, :]
        scores = jnp.einsum('rkgd,tkd->rkgt', query_block.astype(jnp.float32), key_all) * factor
        largest = lax.optimization_barrier(jnp.max(jnp.where(allowed, scores, -1e+30), axis=-1, keepdims=True))
        weights = jnp.where(allowed, jnp.exp(scores - largest), 0.0)
        summed = lax.optimization_barrier(jnp.sum(weights, axis=-1, keepdims=True))
        rounded = lax.optimization_barrier(weights.astype(jnp.bfloat16)).astype(jnp.float32)
        mixed_out = jnp.einsum('rkgt,tkd->rkgd', rounded, value_all) / jnp.maximum(summed, 1.0)
        return mixed_out.astype(jnp.bfloat16).reshape(rows_per_block, QUERY_HEAD_COUNT * HEAD_SIZE)
    return lax.map(one_block, (blocked_queries, mask_blocks)).reshape(TOKENS, QUERY_HEAD_COUNT * HEAD_SIZE)
```

```python
import functools
import math

import jax
import jax.numpy as jnp
from jax import lax
from jax.experimental import pallas as pl
from jax.experimental.pallas import tpu as pltpu
from jax.sharding import PartitionSpec as P

EPSILON = 1e-05
FLOOR_SCORE = -1e30
KV_TOTAL = 1280


def swapped(value, axis, bit):
    mask = 2**bit
    pairs = [(source, source ^ mask) for source in range(lax.axis_size(axis))]
    return lax.ppermute(value, axis, pairs)


def project(chunk_ids, vis_feats, kv_weight, chunk_count, pair):
    rows, width = vis_feats.shape
    wanted = chunk_ids.shape[0]
    kv_heads = kv_weight.shape[1] // pair
    per_kv = chunk_count // kv_heads
    block_rows = rows // per_kv

    def kernel(ids_ref, feats_ref, weight_ref, out_ref):
        out_ref[0] = jnp.dot(feats_ref[...], weight_ref[...], preferred_element_type=jnp.float32)

    return pl.pallas_call(
        kernel,
        grid_spec=pltpu.PrefetchScalarGridSpec(
            num_scalar_prefetch=1,
            grid=(wanted,),
            in_specs=[
                pl.BlockSpec((block_rows, width), lambda n, ids: (ids[n] % per_kv, 0)),
                pl.BlockSpec((width, pair), lambda n, ids: (0, ids[n] // per_kv)),
            ],
            out_specs=pl.BlockSpec((1, block_rows, pair), lambda n, ids: (n, 0, 0)),
        ),
        out_shape=jax.ShapeDtypeStruct((wanted, block_rows, pair), jnp.float32),
        name="project",
    )(chunk_ids, vis_feats, kv_weight)


def finish_chunk(scalars, own, from_left, from_right, key_gain):
    rows, width = own.shape
    head_dim = width // 2
    half = KV_TOTAL // 2
    pieces = len(from_left)

    def kernel(*refs):
        scalars_ref, own_ref = refs[:2]
        left_refs = refs[2 : 2 + pieces]
        right_refs = refs[2 + pieces : 2 + 2 * pieces]
        gain_ref, out_ref = refs[2 + 2 * pieces :]
        sub = rows // pieces
        placed = []
        for piece in range(pieces):
            total = own_ref[piece * sub : (piece + 1) * sub, :] + left_refs[piece][...]
            total = total + right_refs[piece][...]
            raw = total[:, :head_dim]
            mean = jnp.mean(raw * raw, axis=-1, keepdims=True)
            keys = raw * lax.rsqrt(mean + EPSILON) * gain_ref[...]
            placed.append(jnp.concatenate([keys, total[:, head_dim:]], axis=1).astype(jnp.bfloat16))
        data = jnp.concatenate(placed, axis=0)
        start, count, first = scalars_ref[0], scalars_ref[1], scalars_ref[2]
        token = lax.broadcasted_iota(jnp.int32, (half, rows), 1) + first
        token = jnp.where(token < count, token, -2 * KV_TOTAL)
        row = lax.broadcasted_iota(jnp.int32, (half, rows), 0)
        for part in range(2):
            match = (row + (scalars_ref[3 + part] - start)) == token
            chosen = jnp.where(match, 1.0, 0.0).astype(jnp.bfloat16)
            out = jnp.dot(chosen, data, preferred_element_type=jnp.float32)
            out_ref[part] = out.astype(jnp.bfloat16)

    vmem = pl.BlockSpec(memory_space=pltpu.VMEM)
    return pl.pallas_call(
        kernel,
        in_specs=[pl.BlockSpec(memory_space=pltpu.SMEM)] + [vmem] * (2 + 2 * pieces),
        out_specs=vmem,
        out_shape=jax.ShapeDtypeStruct((2, half, width), jnp.bfloat16),
        name="finish",
    )(scalars, own, *from_left, *from_right, key_gain[None, :])


def attend(head_ids, blocks, queries, row_mask, token_bias, previous):
    rows, width = queries.shape
    count = len(blocks)
    half = KV_TOTAL // 2
    head_dim = blocks[0][0].shape[1] // 2
    group = width // (head_dim * attend.kv_heads)
    block_width = group * head_dim
    factor = head_dim ** (-0.5) * math.log2(math.e)
    stack = 2

    def kernel(*refs):
        ids_ref, queries_ref, mask_ref, bias_ref = refs[:4]
        block_refs = refs[4 : 4 + 2 * count]
        refs = refs[4 + 2 * count :]
        if previous is not None:
            refs = refs[1:]
        out_ref, keys_ref, values_ref, query_ref, result_ref, sems = refs
        keys_ref[:, head_dim:] = bias_ref[...]
        some = jnp.min(mask_ref[:, : attend.images].astype(jnp.float32), axis=1, keepdims=True) < 0.5
        for n in range(count):

            @pl.when(ids_ref[n] >= 0)
            def _():
                column = pl.multiple_of(ids_ref[n] * block_width, block_width)
                fetch = pltpu.make_async_copy(
                    queries_ref.at[:, pl.ds(column, block_width)], query_ref, sems.at[0]
                )
                fetch.start()
                for side in range(2):
                    span = slice(side * half, (side + 1) * half)
                    keys_ref[span, :head_dim] = block_refs[2 * n + side][:, :head_dim]
                    values_ref[span, :] = block_refs[2 * n + side][:, head_dim:]
                fetch.wait()
                for first in range(0, group, stack):
                    left = jnp.concatenate(
                        [
                            jnp.concatenate(
                                [query_ref[:, j * head_dim : (j + 1) * head_dim], mask_ref[...]],
                                axis=1,
                            )
                            for j in range(first, first + stack)
                        ],
                        axis=0,
                    )
                    scores = lax.dot_general(
                        left,
                        keys_ref[...],
                        (((1,), (1,)), ((), ())),
                        preferred_element_type=jnp.float32,
                    )
                    largest = jnp.max(scores, axis=1, keepdims=True)
                    weights = jnp.exp2((scores - largest) * factor)
                    summed = jnp.sum(weights, axis=1, keepdims=True)
                    mixed = jnp.dot(
                        weights.astype(jnp.bfloat16),
                        values_ref[...],
                        preferred_element_type=jnp.float32,
                    )
                    mixed = mixed / jnp.maximum(summed, 1.0)
                    for j in range(stack):
                        one = jnp.where(some, mixed[j * rows : (j + 1) * rows], 0.0)
                        at = (first + j) * head_dim
                        result_ref[:, at : at + head_dim] = one.astype(jnp.bfloat16)
                store = pltpu.make_async_copy(
                    result_ref, out_ref.at[:, pl.ds(column, block_width)], sems.at[1]
                )
                store.start()
                store.wait()

    vmem = pl.BlockSpec(memory_space=pltpu.VMEM)
    anywhere = pl.BlockSpec(memory_space=pl.ANY)
    operands = [head_ids, queries, row_mask, token_bias]
    in_specs = [pl.BlockSpec(memory_space=pltpu.SMEM), anywhere, vmem, vmem]
    for mine, other in blocks:
        operands += [mine, other]
        in_specs += [vmem, vmem]
    aliases = {}
    if previous is not None:
        aliases = {len(operands): 0}
        operands.append(previous)
        in_specs.append(anywhere)
    return pl.pallas_call(
        kernel,
        in_specs=in_specs,
        out_specs=anywhere,
        out_shape=jax.ShapeDtypeStruct((rows, width), jnp.bfloat16),
        scratch_shapes=[
            pltpu.VMEM((2 * half, 2 * head_dim), jnp.bfloat16),
            pltpu.VMEM((2 * half, head_dim), jnp.bfloat16),
            pltpu.VMEM((rows, block_width), jnp.bfloat16),
            pltpu.VMEM((rows, block_width), jnp.bfloat16),
            pltpu.SemaphoreType.DMA((2,)),
        ],
        input_output_aliases=aliases,
        name="attend",
    )(*operands)


def sum_over_head(vis_feats, kv_weight, pair, pieces):
    count = lax.axis_size("head")
    here = lax.axis_index("head")
    first = project((count - 1 - here)[None].astype(jnp.int32), vis_feats, kv_weight, count, pair)
    parts = project(jnp.arange(count, dtype=jnp.int32), vis_feats, kv_weight, count, pair)
    sub = parts.shape[1] // pieces

    def part(index, piece):
        index = jnp.clip(index, 0, count - 1)
        cut = lax.dynamic_slice(parts, (index, piece * sub, 0), (1, sub, parts.shape[2]))
        return cut[0]

    to_right, to_left = [None] * pieces, [None] * pieces
    for hop in range(1, count):
        right_pairs = [(i, i + 1) for i in range(min(hop, count - 1))]
        left_pairs = [(count - 1 - i, count - 2 - i) for i in range(min(hop, count - 1))]
        for piece in range(pieces):
            if hop == 1:
                cut = first[0, piece * sub : (piece + 1) * sub]
                right, left = cut, cut
            else:
                right = part(here + count - hop, piece) + to_right[piece]
                left = part(here - count + hop, piece) + to_left[piece]
            to_right[piece] = lax.ppermute(right, "head", right_pairs)
            to_left[piece] = lax.ppermute(left, "head", left_pairs)
    own = lax.dynamic_slice(parts, (here, 0, 0), (1,) + parts.shape[1:])[0]
    return own, to_right, to_left


def shards(queries, vis_feats, kv_weight, key_gain, cross_mask, image_tokens, image_owner):
    head_count = lax.axis_size("head")
    head_index = lax.axis_index("head")
    ctx_index = lax.axis_index("ctx")
    ctx_bits = lax.axis_size("ctx").bit_length() - 1
    images = image_owner.shape[0]
    head_dim = key_gain.shape[0]
    kv_heads = kv_weight.shape[1] // (2 * head_dim)
    per_kv = head_count // kv_heads
    rows = queries.shape[0]
    half = KV_TOTAL // 2

    own, from_left, from_right = sum_over_head(vis_feats, kv_weight, 2 * head_dim, 2)

    ends = jnp.cumsum(image_tokens)
    starts = ends - image_tokens
    mine = image_owner == ctx_index
    core = ctx_index % 2
    scalars = jnp.stack(
        [
            jnp.sum(jnp.where(mine, starts, 0)),
            jnp.sum(jnp.where(mine, image_tokens, 0)),
            (head_index % per_kv) * own.shape[0],
            half * core,
            half * (1 - core),
        ]
    ).astype(jnp.int32)
    packed = finish_chunk(scalars, own, from_left, from_right, key_gain)
    if per_kv > 1:
        groups = [[k * per_kv + j for j in range(per_kv)] for k in range(kv_heads)]
        packed = lax.psum(packed, "head", axis_index_groups=groups)
    block = packed[0] + swapped(packed[1], "ctx", 0)
    keys, values = block[:, :head_dim], block[:, head_dim:]
    for step in range(1, ctx_bits):
        keys = keys + swapped(keys, "ctx", step)
        values = values + swapped(values, "ctx", ctx_bits - step)
    block = jnp.concatenate([keys, values], axis=1)

    row_slice = lax.dynamic_slice_in_dim(cross_mask, head_index * rows, rows, 0)
    row_mask = jnp.concatenate(
        [1.0 - row_slice.astype(jnp.float32), jnp.ones((rows, 1), jnp.float32)], axis=1
    )
    row_mask = jnp.pad(row_mask, ((0, 0), (0, head_dim - images - 1))).astype(jnp.bfloat16)
    position = (jnp.arange(KV_TOTAL, dtype=jnp.int32) + half * core) % KV_TOTAL
    inside = (position[:, None] >= starts[None]) & (position[:, None] < ends[None])
    inside = jnp.concatenate([inside, position[:, None] >= ends[None, -1:]], axis=1)
    token_bias = jnp.where(inside, FLOOR_SCORE, 0.0)
    token_bias = jnp.pad(token_bias, ((0, 0), (0, head_dim - images - 1))).astype(jnp.bfloat16)

    attend.kv_heads = kv_heads
    attend.images = images
    run = functools.partial(
        attend, queries=queries, row_mask=row_mask, token_bias=token_bias
    )
    if per_kv > 1:
        groups = [[k * per_kv + j for k in range(kv_heads)] for j in range(per_kv)]
        gathered = lax.all_gather(block, "head", axis_index_groups=groups)
        other = swapped(gathered, "ctx", 0)
        out = None
        for k in range(kv_heads):
            ids = jnp.full((1,), k, jnp.int32)
            out = run(ids, [(gathered[k], other[k])], previous=out)
        return out

    to_right, to_left = block, block
    arrived = [([head_index], [block])]
    for hop in range(1, head_count):
        right_pairs = [(i, i + 1) for i in range(hop - 1, head_count - 1)]
        left_pairs = [(head_count - 1 - i, head_count - 2 - i) for i, _ in right_pairs]
        to_right = lax.ppermute(to_right, "head", right_pairs)
        to_left = lax.ppermute(to_left, "head", left_pairs)
        below, above = head_index - hop, head_index + hop
        above = jnp.where(above < head_count, above, -1)
        arrived.append(([below, above], [to_right, to_left]))
    out = None
    for ids, blocks in arrived:
        pairs = [(one, swapped(one, "ctx", 0)) for one in blocks]
        out = run(jnp.stack(ids).astype(jnp.int32), pairs, previous=out)
    return out


def solution(mesh):
    return jax.shard_map(
        shards,
        mesh=mesh,
        in_specs=(
            P(("ctx", "head"), None),
            P("ctx", "head"),
            P("head", None),
            P(),
            P("ctx", None),
            P(),
            P(),
        ),
        out_specs=P(("ctx", "head"), None),
        check_vma=False,
    )
```

```python
import math

import jax
import jax.numpy as jnp
from jax import lax
from jax.experimental import pallas as pl
from jax.experimental.pallas import tpu as pltpu
from jax.sharding import PartitionSpec as P

EPSILON = 1e-05
FLOOR_SCORE = -1e30
KV_TOTAL = 1280
PIECES = 2
MIB = 2**20

VMEM = pl.BlockSpec(memory_space=pltpu.VMEM)
SMEM = pl.BlockSpec(memory_space=pltpu.SMEM)
ANYWHERE = pl.BlockSpec(memory_space=pl.ANY)


def params(mib):
    return pltpu.CompilerParams(vmem_limit_bytes=mib * MIB)


def swapped(value, axis, bit):
    mask = 2**bit
    pairs = [(source, source ^ mask) for source in range(lax.axis_size(axis))]
    return lax.ppermute(value, axis, pairs)


def project(chunk_ids, vis_feats, kv_weight, chunk_count, pair):
    rows, width = vis_feats.shape
    wanted = chunk_ids.shape[0]
    per_kv = chunk_count // (kv_weight.shape[1] // pair)
    block_rows = rows // per_kv
    sub = block_rows // PIECES

    def kernel(ids_ref, feats_ref, weight_ref, *refs):
        out_refs, (buffer, sems) = refs[: wanted * PIECES], refs[wanted * PIECES :]

        def fetch(n):
            column = pl.multiple_of((ids_ref[n] // per_kv) * pair, pair)
            return pltpu.make_async_copy(
                weight_ref.at[:, pl.ds(column, pair)], buffer.at[n % 2], sems.at[n % 2]
            )

        fetch(0).start()
        for n in range(wanted):
            if n + 1 < wanted:
                fetch(n + 1).start()
            fetch(n).wait()
            for piece in range(PIECES):
                row = (ids_ref[n] % per_kv) * block_rows + piece * sub if per_kv > 1 else piece * sub
                row = row if per_kv == 1 else pl.multiple_of(row, sub)
                out_refs[n * PIECES + piece][...] = jnp.dot(
                    feats_ref[pl.ds(row, sub), :], buffer[n % 2], preferred_element_type=jnp.float32
                )

    flat = pl.pallas_call(
        kernel,
        in_specs=[SMEM, VMEM, ANYWHERE],
        out_specs=[VMEM] * (wanted * PIECES),
        out_shape=[jax.ShapeDtypeStruct((sub, pair), jnp.float32)] * (wanted * PIECES),
        scratch_shapes=[
            pltpu.VMEM((2, width, pair), kv_weight.dtype),
            pltpu.SemaphoreType.DMA((2,)),
        ],
        compiler_params=params(16),
        cost_estimate=pl.CostEstimate(
            flops=2 * wanted * block_rows * width * pair,
            bytes_accessed=wanted * width * pair * 2,
            transcendentals=0,
        ),
        name="project",
    )(chunk_ids, vis_feats, kv_weight)
    return [flat[n * PIECES : (n + 1) * PIECES] for n in range(wanted)]


def sum_over_head(vis_feats, kv_weight, pair):
    count = lax.axis_size("head")
    here = lax.axis_index("head")

    def parts_at(offsets):
        ids = jnp.stack([(here + offset) % count for offset in offsets]).astype(jnp.int32)
        return dict(zip(offsets, project(ids, vis_feats, kv_weight, count, pair)))

    ends = project((count - 1 - here)[None].astype(jnp.int32), vis_feats, kv_weight, count, pair)[0]
    parts = {}
    for hop in list(range(2, count)) + [count]:
        fresh = [o % count for o in dict.fromkeys((count - hop, hop)) if o % count not in parts]
        if hop == 2 or count > 4:
            if fresh:
                parts.update(parts_at(fresh))
        elif hop == 3:
            parts.update(parts_at(fresh + [0]))
    if 0 not in parts:
        parts.update(parts_at([0]))

    to_right, to_left = [None] * PIECES, [None] * PIECES
    for hop in range(1, count):
        senders = range(min(hop, count - 1))
        right_pairs = [(i, i + 1) for i in senders]
        left_pairs = [(count - 1 - i, count - 2 - i) for i in senders]
        for piece in range(PIECES):
            if hop == 1 and count > 3:
                arrived = lax.ppermute(ends[piece], "head", right_pairs + left_pairs)
                to_right[piece] = to_left[piece] = arrived
                continue
            if hop == 1:
                right = left = ends[piece]
            elif hop == 2 and count == 4:
                right = left = parts[2][piece] + to_right[piece]
            else:
                right = parts[count - hop][piece] + to_right[piece]
                left = parts[hop][piece] + to_left[piece]
            to_right[piece] = lax.ppermute(right, "head", right_pairs)
            to_left[piece] = lax.ppermute(left, "head", left_pairs)
    return parts[0], to_right, to_left


def finish_chunk(own, from_left, from_right, key_gain, image_tokens, image_owner, per_kv):
    rows, width = own[0].shape
    rows = rows * PIECES
    head_dim = width // 2
    half = KV_TOTAL // 2
    images = image_owner.shape[0]
    place = jnp.stack([lax.axis_index("ctx"), lax.axis_index("head") % per_kv]).astype(jnp.int32)

    def kernel(*refs):
        place_ref, tokens_ref, owner_ref = refs[:3]
        own_refs = refs[3 : 3 + PIECES]
        left_refs = refs[3 + PIECES : 3 + 2 * PIECES]
        right_refs = refs[3 + 2 * PIECES : 3 + 3 * PIECES]
        gain_ref, mine_ref, other_ref = refs[3 + 3 * PIECES :]
        placed = []
        for piece in range(PIECES):
            total = own_refs[piece][...] + left_refs[piece][...] + right_refs[piece][...]
            raw = total[:, :head_dim]
            mean = jnp.mean(raw * raw, axis=-1, keepdims=True)
            keys = raw * lax.rsqrt(mean + EPSILON) * gain_ref[...]
            placed.append(jnp.concatenate([keys, total[:, head_dim:]], axis=1).astype(jnp.bfloat16))
        data = jnp.concatenate(placed, axis=0)
        ctx = place_ref[0]
        start, count, before = jnp.int32(0), jnp.int32(0), jnp.int32(0)
        for i in range(images):
            here = owner_ref[i] == ctx
            start = jnp.where(here, before, start)
            count = jnp.where(here, tokens_ref[i], count)
            before = before + tokens_ref[i]
        token = lax.broadcasted_iota(jnp.int32, (half, rows), 1) + place_ref[1] * rows
        token = jnp.where(token < count, token, -2 * KV_TOTAL)
        row = lax.broadcasted_iota(jnp.int32, (half, rows), 0)
        core = ctx % 2
        for ref, side in ((other_ref, 1 - core), (mine_ref, core)):
            match = (row + (side * half - start)) == token
            chosen = jnp.where(match, 1.0, 0.0).astype(jnp.bfloat16)
            ref[...] = jnp.dot(chosen, data, preferred_element_type=jnp.float32).astype(jnp.bfloat16)

    return pl.pallas_call(
        kernel,
        in_specs=[SMEM] * 3 + [VMEM] * (3 * PIECES + 1),
        out_specs=[VMEM] * 2,
        out_shape=[jax.ShapeDtypeStruct((half, width), jnp.bfloat16)] * 2,
        compiler_params=params(16),
        cost_estimate=pl.CostEstimate(
            flops=4 * half * rows * width, bytes_accessed=12 * rows * width, transcendentals=0
        ),
        name="finish",
    )(place, image_tokens, image_owner, *own, *from_left, *from_right, key_gain[None, :])


def mask_columns(cross_mask, image_tokens, head_dim, rows):
    images = image_tokens.shape[0]
    row_slice = lax.dynamic_slice_in_dim(cross_mask, lax.axis_index("head") * rows, rows, 0)
    row_mask = jnp.pad(
        1.0 - row_slice.astype(jnp.float32), ((0, 0), (0, head_dim - images)), constant_values=1.0
    ).astype(jnp.bfloat16)

    def kernel(tokens_ref, out_ref):
        row = lax.broadcasted_iota(jnp.int32, out_ref.shape, 0)
        column = lax.broadcasted_iota(jnp.int32, out_ref.shape, 1)
        before = jnp.int32(0)
        bias = jnp.zeros(out_ref.shape, jnp.float32)
        for i in range(images + 1):
            after = before + tokens_ref[i] if i < images else jnp.int32(KV_TOTAL)
            inside = (column == i) & (row >= before) & (row < after)
            bias = jnp.where(inside, FLOOR_SCORE, bias)
            before = after
        out_ref[...] = bias.astype(jnp.bfloat16)

    token_bias = pl.pallas_call(
        kernel,
        in_specs=[SMEM],
        out_specs=VMEM,
        out_shape=jax.ShapeDtypeStruct((KV_TOTAL, head_dim), jnp.bfloat16),
        compiler_params=params(8),
        name="token_bias",
    )(image_tokens)
    return row_mask, token_bias


def attend(head_ids, blocks, queries, row_mask, token_bias, kv_heads, images, previous):
    rows, width = queries.shape
    count = len(blocks)
    head_dim = blocks[0].shape[1] // 2
    block_width = width // kv_heads
    group = block_width // head_dim
    factor = head_dim ** (-0.5) * math.log2(math.e)
    stack = min(2, group)

    def kernel(*refs):
        ids_ref, queries_ref, mask_ref, bias_ref = refs[:4]
        block_refs = refs[4 : 4 + count]
        out_ref, keys_ref, query_ref, result_ref, sems = refs[4 + count + (previous is not None) :]
        keys_ref[:, head_dim:] = bias_ref[...]
        some = jnp.min(mask_ref[:, :images].astype(jnp.float32), axis=1, keepdims=True) < 0.5
        for n in range(count):

            @pl.when(ids_ref[n] >= 0)
            def _():
                column = pl.multiple_of(ids_ref[n] * block_width, block_width)
                fetch = pltpu.make_async_copy(
                    queries_ref.at[:, pl.ds(column, block_width)], query_ref, sems.at[0]
                )
                fetch.start()
                keys_ref[:, :head_dim] = block_refs[n][:, :head_dim]
                fetch.wait()
                for first in range(0, group, stack):
                    left = jnp.concatenate(
                        [
                            jnp.concatenate(
                                [query_ref[:, j * head_dim : (j + 1) * head_dim], mask_ref[...]],
                                axis=1,
                            )
                            for j in range(first, first + stack)
                        ],
                        axis=0,
                    )
                    scores = lax.dot_general(
                        left,
                        keys_ref[...],
                        (((1,), (1,)), ((), ())),
                        preferred_element_type=jnp.float32,
                    )
                    largest = jnp.max(scores, axis=1, keepdims=True)
                    weights = jnp.exp2((scores - largest) * factor)
                    summed = jnp.sum(weights, axis=1, keepdims=True)
                    mixed = jnp.dot(
                        weights.astype(jnp.bfloat16),
                        block_refs[n][:, head_dim:],
                        preferred_element_type=jnp.float32,
                    )
                    mixed = mixed / jnp.maximum(summed, 1.0)
                    for j in range(stack):
                        one = jnp.where(some, mixed[j * rows : (j + 1) * rows], 0.0)
                        at = (first + j) * head_dim
                        result_ref[:, at : at + head_dim] = one.astype(jnp.bfloat16)
                store = pltpu.make_async_copy(
                    result_ref, out_ref.at[:, pl.ds(column, block_width)], sems.at[1]
                )
                store.start()
                store.wait()

    operands = [head_ids, queries, row_mask, token_bias, *blocks]
    in_specs = [SMEM, ANYWHERE] + [VMEM] * (2 + count)
    aliases = {}
    if previous is not None:
        aliases = {len(operands): 0}
        operands.append(previous)
        in_specs.append(ANYWHERE)
    return pl.pallas_call(
        kernel,
        in_specs=in_specs,
        out_specs=ANYWHERE,
        out_shape=jax.ShapeDtypeStruct((rows, width), jnp.bfloat16),
        scratch_shapes=[
            pltpu.VMEM((KV_TOTAL, 2 * head_dim), jnp.bfloat16),
            pltpu.VMEM((rows, block_width), jnp.bfloat16),
            pltpu.VMEM((rows, block_width), jnp.bfloat16),
            pltpu.SemaphoreType.DMA((2,)),
        ],
        input_output_aliases=aliases,
        compiler_params=params(24),
        cost_estimate=pl.CostEstimate(
            flops=6 * count * rows * group * KV_TOTAL * head_dim,
            bytes_accessed=count * rows * block_width * 4,
            transcendentals=count * rows * group * KV_TOTAL,
        ),
        name="attend",
    )(*operands)


def shards(queries, vis_feats, kv_weight, key_gain, cross_mask, image_tokens, image_owner):
    head_count = lax.axis_size("head")
    head_index = lax.axis_index("head")
    ctx_count = lax.axis_size("ctx")
    core = lax.axis_index("ctx") % 2
    ctx_bits = ctx_count.bit_length() - 1
    head_dim = key_gain.shape[0]
    kv_heads = kv_weight.shape[1] // (2 * head_dim)
    per_kv = head_count // kv_heads
    rows = queries.shape[0]

    row_mask, token_bias = mask_columns(cross_mask, image_tokens, head_dim, rows)
    own, from_left, from_right = sum_over_head(vis_feats, kv_weight, 2 * head_dim)
    block, other = finish_chunk(
        own, from_left, from_right, key_gain, image_tokens, image_owner, per_kv
    )
    if per_kv > 1:
        groups = [[k * per_kv + j for j in range(per_kv)] for k in range(kv_heads)]
        block, other = lax.psum((block, other), "head", axis_index_groups=groups)

    block = block + swapped(other, "ctx", 0)
    for step in range(1, ctx_bits):
        pairs = [(c, c ^ (2**step if c % 2 == 0 else 2 ** (ctx_bits - step))) for c in range(ctx_count)]
        block = block + lax.ppermute(block, "ctx", pairs)
    other = swapped(block, "ctx", 0)
    block = jnp.where(
        core == 0, jnp.concatenate([block, other], 0), jnp.concatenate([other, block], 0)
    )

    def run(ids, blocks, previous):
        ids = jnp.stack(ids).astype(jnp.int32)
        return attend(
            ids, blocks, queries, row_mask, token_bias, kv_heads, image_tokens.shape[0], previous
        )

    if per_kv > 1:
        groups = [[k * per_kv + j for k in range(kv_heads)] for j in range(per_kv)]
        gathered = lax.all_gather(block, "head", axis_index_groups=groups)
        out = None
        for k in range(kv_heads):
            out = run([jnp.int32(k)], [gathered[k]], out)
        return out

    def place(c, h):
        return c * head_count + h

    out = run([head_index], [block], None)
    passing = block
    side = 1 - 2 * core
    for hop in range(1, head_count):
        pairs = []
        for c in range(ctx_count):
            for i in range(hop - 1, head_count - 1):
                if c % 2 == 0:
                    pairs.append((place(c, i), place(c, i + 1)))
                else:
                    pairs.append((place(c, head_count - 1 - i), place(c, head_count - 2 - i)))
        passing = lax.ppermute(passing, ("ctx", "head"), pairs)
        passing, out = lax.optimization_barrier((passing, out))
        ids = [head_index - hop * side, head_index + hop * side]
        ids = [jnp.where((i >= 0) & (i < head_count), i, -1) for i in ids]
        out = run(ids, [passing, swapped(passing, "ctx", 0)], out)
    return out


def solution(mesh):
    return jax.shard_map(
        shards,
        mesh=mesh,
        in_specs=(
            P(("ctx", "head"), None),
            P("ctx", "head"),
            P("head", None),
            P(),
            P("ctx", None),
            P(),
            P(),
        ),
        out_specs=P(("ctx", "head"), None),
        check_vma=False,
    )
```

```python
import math

import jax
import jax.numpy as jnp
from jax import lax
from jax.experimental import pallas as pl
from jax.experimental.pallas import tpu as pltpu
from jax.sharding import PartitionSpec as P

EPSILON = 1e-05
FLOOR_SCORE = -1e30
KV_TOTAL = 1280
STACK = 2
MIB = 2**20

VMEM = pl.BlockSpec(memory_space=pltpu.VMEM)
SMEM = pl.BlockSpec(memory_space=pltpu.SMEM)
ANYWHERE = pl.BlockSpec(memory_space=pl.ANY)
HBM = pl.BlockSpec(memory_space=pltpu.HBM)


def params(mib):
    return pltpu.CompilerParams(vmem_limit_bytes=mib * MIB)


def swapped(value, axis, bit):
    mask = 2**bit
    pairs = [(source, source ^ mask) for source in range(lax.axis_size(axis))]
    return lax.ppermute(value, axis, pairs)


def project(chunk_ids, vis_feats, kv_weight, chunk_count, pair):
    rows, width = vis_feats.shape
    wanted = chunk_ids.shape[0]
    per_kv = chunk_count // (kv_weight.shape[1] // pair)
    block_rows = rows // per_kv
    head_dim = pair // 2
    columns = pair if wanted == 1 else kv_weight.shape[1]
    steps = 4
    few, deep = rows // steps, width // steps

    def kernel(ids_ref, feats_hbm, weight_hbm, *refs):
        out_refs, (feats_ref, weight_ref, sems) = refs[: 2 * wanted], refs[2 * wanted :]
        copies = []
        for n in range(steps):
            span = pl.ds(n * few, few)
            copies.append((feats_hbm.at[span], feats_ref.at[span], sems.at[n]))
        first = pl.multiple_of((ids_ref[0] // per_kv) * pair, pair)
        for n in range(steps):
            span = pl.ds(n * deep, deep)
            source = weight_hbm.at[span, pl.ds(first, pair)] if wanted == 1 else weight_hbm.at[span]
            copies.append((source, weight_ref.at[span], sems.at[steps + n]))
        copies = [pltpu.make_async_copy(*copy) for copy in copies]
        for copy in copies:
            copy.start()
        for copy in copies:
            copy.wait()
        for n in range(wanted):
            column = 0 if wanted == 1 else pl.multiple_of((ids_ref[n] // per_kv) * pair, pair)
            row = 0 if per_kv == 1 else pl.multiple_of((ids_ref[n] % per_kv) * block_rows, block_rows)
            out = jnp.dot(
                feats_ref[pl.ds(row, block_rows), :],
                weight_ref[:, pl.ds(column, pair)],
                preferred_element_type=jnp.float32,
            )
            out_refs[2 * n][...] = out[:, :head_dim]
            out_refs[2 * n + 1][...] = out[:, head_dim:]

    flat = pl.pallas_call(
        kernel,
        in_specs=[SMEM, HBM, HBM],
        out_specs=[VMEM] * (2 * wanted),
        out_shape=[jax.ShapeDtypeStruct((block_rows, head_dim), jnp.float32)] * (2 * wanted),
        scratch_shapes=[
            pltpu.VMEM((rows, width), vis_feats.dtype),
            pltpu.VMEM((width, columns), kv_weight.dtype),
            pltpu.SemaphoreType.DMA((2 * steps,)),
        ],
        compiler_params=params(16),
        cost_estimate=pl.CostEstimate(
            flops=2 * wanted * block_rows * width * pair,
            bytes_accessed=(columns + rows) * width * 2,
            transcendentals=0,
        ),
        name="project",
    )(
        chunk_ids,
        pltpu.with_memory_space_constraint(vis_feats, pltpu.HBM),
        pltpu.with_memory_space_constraint(kv_weight, pltpu.HBM),
    )
    return [flat[2 * n : 2 * n + 2] for n in range(wanted)]


def project_rest(chunk_ids, vis_feats, kv_weight, chunk_count, pair):
    rows, width = vis_feats.shape
    wanted = chunk_ids.shape[0]
    per_kv = chunk_count // (kv_weight.shape[1] // pair)
    block_rows = rows // per_kv
    head_dim = pair // 2

    def kernel(ids_ref, feats_ref, weight_ref, *out_refs):
        for n in range(wanted):
            column = pl.multiple_of((ids_ref[n] // per_kv) * pair, pair)
            row = 0 if per_kv == 1 else pl.multiple_of((ids_ref[n] % per_kv) * block_rows, block_rows)
            out = jnp.dot(
                feats_ref[pl.ds(row, block_rows), :],
                weight_ref[:, pl.ds(column, pair)],
                preferred_element_type=jnp.float32,
            )
            out_refs[2 * n][...] = out[:, :head_dim]
            out_refs[2 * n + 1][...] = out[:, head_dim:]

    flat = pl.pallas_call(
        kernel,
        in_specs=[SMEM, VMEM, VMEM],
        out_specs=[VMEM] * (2 * wanted),
        out_shape=[jax.ShapeDtypeStruct((block_rows, head_dim), jnp.float32)] * (2 * wanted),
        compiler_params=params(8),
        cost_estimate=pl.CostEstimate(
            flops=2 * wanted * block_rows * width * pair,
            bytes_accessed=wanted * pair * width * 2,
            transcendentals=0,
        ),
        name="project_rest",
    )(chunk_ids, vis_feats, kv_weight)
    return [flat[2 * n : 2 * n + 2] for n in range(wanted)]


def sum_over_head(vis_feats, kv_weight, pair, early):
    count = lax.axis_size("head")
    here = lax.axis_index("head")
    first = (count - 1 - here)[None].astype(jnp.int32)
    ends = project(first, vis_feats, kv_weight, count, pair)[0]
    offsets = []
    for hop in range(2, count):
        offsets += [o for o in dict.fromkeys((count - hop, hop)) if o not in offsets]
    offsets.append(0)
    ids = ((here + jnp.array(offsets, jnp.int32)) % count).astype(jnp.int32)
    parts = dict(zip(offsets, project_rest(ids, vis_feats, kv_weight, count, pair)))
    held = lax.optimization_barrier((ends[1], parts[0][0], *early))
    ends = (ends[0], held[0])
    parts[0] = (held[1], parts[0][1])
    early = held[2:]

    to_right, to_left = [None] * 2, [None] * 2
    for hop in range(1, count):
        senders = range(min(hop, count - 1))
        right_pairs = [(i, i + 1) for i in senders]
        left_pairs = [(count - 1 - i, count - 2 - i) for i in senders]
        for piece in range(2):
            if hop == 1 and count > 3:
                arrived = lax.ppermute(ends[piece], "head", right_pairs + left_pairs)
                to_right[piece] = to_left[piece] = arrived
                continue
            if hop == 1:
                right = left = ends[piece]
            elif hop == 2 and count == 4:
                right = left = parts[2][piece] + to_right[piece]
            else:
                right = parts[count - hop][piece] + to_right[piece]
                left = parts[hop][piece] + to_left[piece]
            to_right[piece] = lax.ppermute(right, "head", right_pairs)
            to_left[piece] = lax.ppermute(left, "head", left_pairs)
    return [[parts[0][piece], to_right[piece], to_left[piece]] for piece in range(2)], early


def finish_chunk(partial_sums, key_gain, image_tokens, image_owner, per_kv, are_keys):
    rows, head_dim = partial_sums[0].shape
    half = KV_TOTAL // 2
    images = image_owner.shape[0]
    place = jnp.stack([lax.axis_index("ctx"), lax.axis_index("head") % per_kv]).astype(jnp.int32)

    def kernel(place_ref, tokens_ref, owner_ref, own_ref, left_ref, right_ref, gain_ref, mine_ref, other_ref):
        data = own_ref[...] + left_ref[...] + right_ref[...]
        if are_keys:
            mean = jnp.mean(data * data, axis=-1, keepdims=True)
            data = data * lax.rsqrt(mean + EPSILON) * gain_ref[...]
        data = data.astype(jnp.bfloat16)
        ctx = place_ref[0]
        start, count, before = jnp.int32(0), jnp.int32(0), jnp.int32(0)
        for i in range(images):
            here = owner_ref[i] == ctx
            start = jnp.where(here, before, start)
            count = jnp.where(here, tokens_ref[i], count)
            before = before + tokens_ref[i]
        token = lax.broadcasted_iota(jnp.int32, (half, rows), 1) + place_ref[1] * rows
        token = jnp.where(token < count, token, -2 * KV_TOTAL)
        row = lax.broadcasted_iota(jnp.int32, (half, rows), 0)
        core = ctx % 2
        for ref, side in ((other_ref, 1 - core), (mine_ref, core)):
            match = (row + (side * half - start)) == token
            chosen = jnp.where(match, 1.0, 0.0).astype(jnp.bfloat16)
            ref[...] = jnp.dot(chosen, data, preferred_element_type=jnp.float32).astype(jnp.bfloat16)

    return pl.pallas_call(
        kernel,
        in_specs=[SMEM] * 3 + [VMEM] * 4,
        out_specs=[VMEM] * 2,
        out_shape=[jax.ShapeDtypeStruct((half, head_dim), jnp.bfloat16)] * 2,
        compiler_params=params(16),
        cost_estimate=pl.CostEstimate(
            flops=4 * half * rows * head_dim, bytes_accessed=12 * rows * head_dim, transcendentals=0
        ),
        name="finish",
    )(place, image_tokens, image_owner, *partial_sums, key_gain[None, :])


def mask_columns(cross_mask, image_tokens, head_dim, rows):
    images = image_tokens.shape[0]
    row_slice = lax.dynamic_slice_in_dim(cross_mask, lax.axis_index("head") * rows, rows, 0)
    row_mask = jnp.pad(
        1.0 - row_slice.astype(jnp.float32), ((0, 0), (0, head_dim - images)), constant_values=1.0
    ).astype(jnp.bfloat16)

    def kernel(tokens_ref, out_ref):
        row = lax.broadcasted_iota(jnp.int32, out_ref.shape, 0)
        column = lax.broadcasted_iota(jnp.int32, out_ref.shape, 1)
        before = jnp.int32(0)
        bias = jnp.zeros(out_ref.shape, jnp.float32)
        for i in range(images + 1):
            after = before + tokens_ref[i] if i < images else jnp.int32(KV_TOTAL)
            inside = (column == i) & (row >= before) & (row < after)
            bias = jnp.where(inside, FLOOR_SCORE, bias)
            before = after
        out_ref[...] = bias.astype(jnp.bfloat16)

    token_bias = pl.pallas_call(
        kernel,
        in_specs=[SMEM],
        out_specs=VMEM,
        out_shape=jax.ShapeDtypeStruct((KV_TOTAL, head_dim), jnp.bfloat16),
        compiler_params=params(8),
        name="token_bias",
    )(image_tokens)
    return row_mask, token_bias


def attend(call, own, arrivals, queries, row_mask, token_bias, kv_heads, images, previous):
    rows, width = queries.shape
    tokens, head_dim = own[0].shape
    block_width = width // kv_heads
    group = block_width // head_dim
    factor = head_dim ** (-0.5) * math.log2(math.e)
    stack = min(STACK, group)
    first_hop = (call + 1) // 2
    sources = [own] if call == 0 else [pair for hop in arrivals[first_hop - 1 : call] for pair in hop]
    count = len(sources)
    line = own[2]
    ids = own[3]

    def kernel(*refs):
        ids_ref, queries_ref, mask_ref, bias_ref = refs[:4]
        source_refs = refs[4 : 4 + 2 * count]
        refs = refs[4 + 2 * count + (previous is not None) :]
        out_ref, keys_ref, values_ref, query_ref, result_ref, sems = refs
        here, step = ids_ref[0], ids_ref[1]

        def take(n):
            keys_ref[:, :head_dim] = source_refs[2 * n][...]
            values_ref[...] = source_refs[2 * n + 1][...]

        head = here
        if call == 0:
            take(0)
        else:
            rank = jnp.int32(0)
            for hop in range(1, call + 1):
                for side in range(2):
                    candidate = here + (hop if side else -hop) * step
                    valid = (candidate >= 0) & (candidate < line)
                    rank = rank + jnp.where(valid, 1, 0)
                    chosen = valid & (rank == call)
                    head = jnp.where(chosen, candidate, head)
                    if hop >= first_hop:
                        pl.when(chosen)(lambda n=2 * (hop - first_hop) + side: take(n))
        column = pl.multiple_of(head * block_width, block_width)
        fetch = pltpu.make_async_copy(
            queries_ref.at[:, pl.ds(column, block_width)], query_ref, sems.at[0]
        )
        fetch.start()
        keys_ref[:, head_dim:] = bias_ref[...]
        some = jnp.min(mask_ref[:, :images].astype(jnp.float32), axis=1, keepdims=True) < 0.5
        fetch.wait()
        for first in range(0, group, stack):
            left = jnp.concatenate(
                [
                    jnp.concatenate(
                        [query_ref[:, j * head_dim : (j + 1) * head_dim], mask_ref[...]], axis=1
                    )
                    for j in range(first, first + stack)
                ],
                axis=0,
            )
            scores = lax.dot_general(
                left, keys_ref[...], (((1,), (1,)), ((), ())), preferred_element_type=jnp.float32
            )
            largest = jnp.max(scores, axis=1, keepdims=True)
            weights = jnp.exp2((scores - largest) * factor)
            summed = jnp.sum(weights, axis=1, keepdims=True)
            mixed = jnp.dot(
                weights.astype(jnp.bfloat16), values_ref[...], preferred_element_type=jnp.float32
            )
            mixed = mixed / jnp.maximum(summed, 1.0)
            for j in range(stack):
                one = jnp.where(some, mixed[j * rows : (j + 1) * rows], 0.0)
                at = (first + j) * head_dim
                result_ref[:, at : at + head_dim] = one.astype(jnp.bfloat16)
        store = pltpu.make_async_copy(
            result_ref, out_ref.at[:, pl.ds(column, block_width)], sems.at[1]
        )
        store.start()
        store.wait()

    operands = [ids, queries, row_mask, token_bias]
    for source in sources:
        operands += [source[0], source[1]]
    in_specs = [SMEM, ANYWHERE] + [VMEM] * (len(operands) - 2)
    aliases = {}
    if previous is not None:
        aliases = {len(operands): 0}
        operands.append(previous)
        in_specs.append(ANYWHERE)
    return pl.pallas_call(
        kernel,
        in_specs=in_specs,
        out_specs=ANYWHERE,
        out_shape=jax.ShapeDtypeStruct((rows, width), jnp.bfloat16),
        scratch_shapes=[
            pltpu.VMEM((tokens, 2 * head_dim), jnp.bfloat16),
            pltpu.VMEM((tokens, head_dim), jnp.bfloat16),
            pltpu.VMEM((rows, block_width), jnp.bfloat16),
            pltpu.VMEM((rows, block_width), jnp.bfloat16),
            pltpu.SemaphoreType.DMA((2,)),
        ],
        input_output_aliases=aliases,
        compiler_params=params(24),
        cost_estimate=pl.CostEstimate(
            flops=6 * rows * group * tokens * head_dim,
            bytes_accessed=rows * block_width * 4,
            transcendentals=rows * group * tokens,
        ),
        name="attend",
    )(*operands)


def shards(queries, vis_feats, kv_weight, key_gain, cross_mask, image_tokens, image_owner):
    head_count = lax.axis_size("head")
    head_index = lax.axis_index("head")
    ctx_count = lax.axis_size("ctx")
    core = lax.axis_index("ctx") % 2
    ctx_bits = ctx_count.bit_length() - 1
    head_dim = key_gain.shape[0]
    kv_heads = kv_weight.shape[1] // (2 * head_dim)
    per_kv = head_count // kv_heads
    images = image_tokens.shape[0]

    masks = mask_columns(cross_mask, image_tokens, head_dim, queries.shape[0])
    partial_sums, (row_mask, token_bias) = sum_over_head(vis_feats, kv_weight, 2 * head_dim, masks)

    def spread(piece):
        block, other = finish_chunk(
            partial_sums[piece], key_gain, image_tokens, image_owner, per_kv, piece == 0
        )
        if per_kv > 1:
            groups = [[k * per_kv + j for j in range(per_kv)] for k in range(kv_heads)]
            block, other = lax.psum((block, other), "head", axis_index_groups=groups)
        block = block + swapped(other, "ctx", 0)
        for step in range(1, ctx_bits):
            pairs = [
                (c, c ^ (2**step if c % 2 == 0 else 2 ** (ctx_bits - step))) for c in range(ctx_count)
            ]
            block = block + lax.ppermute(block, "ctx", pairs)
        other = swapped(block, "ctx", 0)
        return jnp.where(
            core == 0, jnp.concatenate([block, other], 0), jnp.concatenate([other, block], 0)
        )

    keys, values = spread(0), spread(1)

    if per_kv > 1:
        groups = [[k * per_kv + j for k in range(kv_heads)] for j in range(per_kv)]
        keys = lax.all_gather(keys, "head", axis_index_groups=groups)
        values = lax.all_gather(values, "head", axis_index_groups=groups)
        out = None
        for k in range(kv_heads):
            ids = jnp.array([k, 1], jnp.int32)
            own = (keys[k], values[k], kv_heads, ids)
            out = attend(0, own, [], queries, row_mask, token_bias, kv_heads, images, out)
        return out

    def place(c, h):
        return c * head_count + h

    own = (keys, values, head_count, jnp.stack([head_index, 1 - 2 * core]).astype(jnp.int32))
    arrivals = []
    out = attend(0, own, arrivals, queries, row_mask, token_bias, kv_heads, images, None)
    passing = [keys, values]
    for hop in range(1, head_count):
        pairs = []
        for c in range(ctx_count):
            for i in range(hop - 1, head_count - 1):
                if c % 2 == 0:
                    pairs.append((place(c, i), place(c, i + 1)))
                else:
                    pairs.append((place(c, head_count - 1 - i), place(c, head_count - 2 - i)))
        crossing = [None, None]
        for piece in range(2):
            passing[piece] = lax.ppermute(passing[piece], ("ctx", "head"), pairs)
            crossing[piece] = swapped(passing[piece], "ctx", 0)
        arrivals.append([tuple(passing), tuple(crossing)])
        out = attend(hop, own, arrivals, queries, row_mask, token_bias, kv_heads, images, out)
    return out


def solution(mesh):
    return jax.shard_map(
        shards,
        mesh=mesh,
        in_specs=(
            P(("ctx", "head"), None),
            P("ctx", "head"),
            P("head", None),
            P(),
            P("ctx", None),
            P(),
            P(),
        ),
        out_specs=P(("ctx", "head"), None),
        check_vma=False,
    )
```

```python
import math

import jax
import jax.numpy as jnp
from jax import lax
from jax.experimental import pallas as pl
from jax.experimental.pallas import tpu as pltpu
from jax.sharding import PartitionSpec as P

EPSILON = 1e-05
FLOOR_SCORE = -1e30
KV_TOTAL = 1280
STACK = 2
MIB = 2**20

VMEM = pl.BlockSpec(memory_space=pltpu.VMEM)
SMEM = pl.BlockSpec(memory_space=pltpu.SMEM)
ANYWHERE = pl.BlockSpec(memory_space=pl.ANY)
HBM = pl.BlockSpec(memory_space=pltpu.HBM)


def params(mib):
    return pltpu.CompilerParams(vmem_limit_bytes=mib * MIB)


def swapped(value, axis, bit):
    mask = 2**bit
    pairs = [(source, source ^ mask) for source in range(lax.axis_size(axis))]
    return lax.ppermute(value, axis, pairs)


def project(chunk_of, wanted, vis_feats, kv_weight, pair):
    count = lax.axis_size("head")
    rows, width = vis_feats.shape
    per_kv = count // (kv_weight.shape[1] // pair)
    block_rows = rows // per_kv
    head_dim = pair // 2
    alone = wanted == 1
    steps = 4
    few, deep = rows // steps, width // steps

    def kernel(feats_ref, weight_ref, *refs):
        out_refs = refs[: 2 * wanted]
        chunks = [chunk_of(lax.axis_index("head"), n) for n in range(wanted)]
        columns = [pl.multiple_of((chunk // per_kv) * pair, pair) for chunk in chunks]
        if alone:
            feats_vmem, weight_vmem, sems = refs[2 * wanted :]
            copies = []
            for n in range(steps):
                span = pl.ds(n * few, few)
                copies.append((feats_ref.at[span], feats_vmem.at[span], sems.at[n]))
            for n in range(steps):
                span = pl.ds(n * deep, deep)
                source = weight_ref.at[span, pl.ds(columns[0], pair)]
                copies.append((source, weight_vmem.at[span], sems.at[steps + n]))
            copies = [pltpu.make_async_copy(*copy) for copy in copies]
            for copy in copies:
                copy.start()
            for copy in copies:
                copy.wait()
            feats_ref, weight_ref, columns = feats_vmem, weight_vmem, [0]
        for n in range(wanted):
            row = 0 if per_kv == 1 else pl.multiple_of((chunks[n] % per_kv) * block_rows, block_rows)
            out = jnp.dot(
                feats_ref[pl.ds(row, block_rows), :],
                weight_ref[:, pl.ds(columns[n], pair)],
                preferred_element_type=jnp.float32,
            )
            out_refs[2 * n][...] = out[:, :head_dim]
            out_refs[2 * n + 1][...] = out[:, head_dim:]

    scratch = [
        pltpu.VMEM((rows, width), vis_feats.dtype),
        pltpu.VMEM((width, pair), kv_weight.dtype),
        pltpu.SemaphoreType.DMA((2 * steps,)),
    ]
    if alone:
        vis_feats = pltpu.with_memory_space_constraint(vis_feats, pltpu.HBM)
        kv_weight = pltpu.with_memory_space_constraint(kv_weight, pltpu.HBM)
    flat = pl.pallas_call(
        kernel,
        in_specs=[HBM, HBM] if alone else [VMEM, VMEM],
        out_specs=[VMEM] * (2 * wanted),
        out_shape=[jax.ShapeDtypeStruct((block_rows, head_dim), jnp.float32)] * (2 * wanted),
        scratch_shapes=scratch if alone else [],
        compiler_params=params(10),
        cost_estimate=pl.CostEstimate(
            flops=2 * wanted * block_rows * width * pair,
            bytes_accessed=(wanted * pair + rows) * width * 2,
            transcendentals=0,
        ),
        name="project",
    )(vis_feats, kv_weight)
    return [flat[2 * n : 2 * n + 2] for n in range(wanted)]


def sum_over_head(vis_feats, kv_weight, pair, early):
    count = lax.axis_size("head")
    ends = project(lambda here, n: count - 1 - here, 1, vis_feats, kv_weight, pair)[0]
    offsets = []
    for hop in range(2, count):
        offsets += [o for o in dict.fromkeys((count - hop, hop)) if o not in offsets]
    offsets.append(0)

    def rest(here, n):
        chunk = here + offsets[n]
        return jnp.where(chunk >= count, chunk - count, chunk)

    parts = dict(zip(offsets, project(rest, len(offsets), vis_feats, kv_weight, pair)))
    held = lax.optimization_barrier((ends[1], parts[0][0], *early))
    ends = (ends[0], held[0])
    parts[0] = (held[1], parts[0][1])
    early = held[2:]

    to_right, to_left = [None] * 2, [None] * 2
    for hop in range(1, count):
        senders = range(min(hop, count - 1))
        right_pairs = [(i, i + 1) for i in senders]
        left_pairs = [(count - 1 - i, count - 2 - i) for i in senders]
        for piece in range(2):
            if hop == 1 and count > 3:
                arrived = lax.ppermute(ends[piece], "head", right_pairs + left_pairs)
                to_right[piece] = to_left[piece] = arrived
                continue
            if hop == 1:
                right = left = ends[piece]
            elif hop == 2 and count == 4:
                right = left = parts[2][piece] + to_right[piece]
            else:
                right = parts[count - hop][piece] + to_right[piece]
                left = parts[hop][piece] + to_left[piece]
            to_right[piece] = lax.ppermute(right, "head", right_pairs)
            to_left[piece] = lax.ppermute(left, "head", left_pairs)
    return [[parts[0][piece], to_right[piece], to_left[piece]] for piece in range(2)], early


def finish_chunk(partial_sums, key_gain, image_tokens, image_owner, per_kv, are_keys):
    rows, head_dim = partial_sums[0].shape
    half = KV_TOTAL // 2
    images = image_owner.shape[0]

    def kernel(tokens_ref, owner_ref, own_ref, left_ref, right_ref, gain_ref, mine_ref, other_ref):
        data = own_ref[...] + left_ref[...] + right_ref[...]
        if are_keys:
            mean = jnp.mean(data * data, axis=-1, keepdims=True)
            data = data * lax.rsqrt(mean + EPSILON) * gain_ref[...]
        data = data.astype(jnp.bfloat16)
        ctx = lax.axis_index("ctx")
        start, count, before = jnp.int32(0), jnp.int32(0), jnp.int32(0)
        for i in range(images):
            here = owner_ref[i] == ctx
            start = jnp.where(here, before, start)
            count = jnp.where(here, tokens_ref[i], count)
            before = before + tokens_ref[i]
        token = lax.broadcasted_iota(jnp.int32, (half, rows), 1) + (lax.axis_index("head") % per_kv) * rows
        token = jnp.where(token < count, token, -2 * KV_TOTAL)
        row = lax.broadcasted_iota(jnp.int32, (half, rows), 0)
        core = ctx % 2
        for ref, side in ((other_ref, 1 - core), (mine_ref, core)):
            match = (row + (side * half - start)) == token
            chosen = jnp.where(match, 1.0, 0.0).astype(jnp.bfloat16)
            ref[...] = jnp.dot(chosen, data, preferred_element_type=jnp.float32).astype(jnp.bfloat16)

    return pl.pallas_call(
        kernel,
        in_specs=[SMEM] * 2 + [VMEM] * 4,
        out_specs=[VMEM] * 2,
        out_shape=[jax.ShapeDtypeStruct((half, head_dim), jnp.bfloat16)] * 2,
        compiler_params=params(16),
        cost_estimate=pl.CostEstimate(
            flops=4 * half * rows * head_dim, bytes_accessed=12 * rows * head_dim, transcendentals=0
        ),
        name="finish",
    )(image_tokens, image_owner, *partial_sums, key_gain[None, :])


def mask_columns(cross_mask, image_tokens, head_dim, rows):
    images = image_tokens.shape[0]

    def kernel(tokens_ref, cross_ref, row_ref, bias_ref):
        here = pl.multiple_of(lax.axis_index("head") * rows, rows)
        cross = cross_ref[pl.ds(here, rows), :].astype(jnp.float32)
        column = lax.broadcasted_iota(jnp.int32, row_ref.shape, 1)
        closed = jnp.ones(row_ref.shape, jnp.float32)
        for i in range(images):
            closed = jnp.where(column == i, 1.0 - cross[:, i : i + 1], closed)
        row_ref[...] = closed.astype(jnp.bfloat16)
        row = lax.broadcasted_iota(jnp.int32, bias_ref.shape, 0)
        column = lax.broadcasted_iota(jnp.int32, bias_ref.shape, 1)
        before = jnp.int32(0)
        bias = jnp.zeros(bias_ref.shape, jnp.float32)
        for i in range(images + 1):
            after = before + tokens_ref[i] if i < images else jnp.int32(KV_TOTAL)
            inside = (column == i) & (row >= before) & (row < after)
            bias = jnp.where(inside, FLOOR_SCORE, bias)
            before = after
        bias_ref[...] = bias.astype(jnp.bfloat16)

    return pl.pallas_call(
        kernel,
        in_specs=[SMEM, VMEM],
        out_specs=[VMEM] * 2,
        out_shape=[
            jax.ShapeDtypeStruct((rows, head_dim), jnp.bfloat16),
            jax.ShapeDtypeStruct((KV_TOTAL, head_dim), jnp.bfloat16),
        ],
        compiler_params=params(8),
        name="masks",
    )(image_tokens, cross_mask)


def attend(call, own, arrivals, queries, row_mask, token_bias, kv_heads, images, previous, key_head=None):
    rows, width = queries.shape
    tokens, head_dim = own[0].shape
    half = tokens // 2
    block_width = width // kv_heads
    group = block_width // head_dim
    factor = head_dim ** (-0.5) * math.log2(math.e)
    stack = min(STACK, group)
    blocks = range(group // stack)
    first_hop = (call + 1) // 2
    sources = [own] if call == 0 else [pair for hop in arrivals[first_hop - 1 : call] for pair in hop]
    count = len(sources)
    line = lax.axis_size("head")

    def kernel(*refs):
        queries_ref, mask_ref, bias_ref = refs[:3]
        source_refs = refs[3 : 3 + 2 * count]
        out_ref, keys_ref, values_ref, result_ref, sem = refs[3 + 2 * count + (previous is not None) :]
        core = lax.axis_index("ctx") % 2
        head = lax.axis_index("head") if key_head is None else key_head

        def take(n, core):
            for side, at in ((0, core), (1, 1 - core)):
                span = pl.ds(pl.multiple_of(at * half, half), half)
                keys_ref[span, :head_dim] = source_refs[2 * n][side * half : (side + 1) * half, :]
                values_ref[span, :] = source_refs[2 * n + 1][side * half : (side + 1) * half, :]

        keys_ref[:, head_dim:] = bias_ref[...]
        if call == 0:
            take(0, core)
        else:
            here, step = head, 1 - 2 * core
            rank = jnp.int32(0)
            for hop in range(1, call + 1):
                for side in range(2):
                    candidate = here + (hop if side else -hop) * step
                    valid = (candidate >= 0) & (candidate < line)
                    rank = rank + jnp.where(valid, 1, 0)
                    chosen = valid & (rank == call)
                    head = jnp.where(chosen, candidate, head)
                    if hop >= first_hop:
                        n = 2 * (hop - first_hop) + side
                        source_core = 1 - core if side else core
                        pl.when(chosen)(lambda n=n, at=source_core: take(n, at))
        column = pl.multiple_of(head * block_width, block_width)
        some = jnp.min(mask_ref[:, :images].astype(jnp.float32), axis=1, keepdims=True) < 0.5

        def scores_of(n):
            left = []
            for j in range(n * stack, (n + 1) * stack):
                query = queries_ref[:, pl.ds(column + j * head_dim, head_dim)]
                left.append(jnp.concatenate([query, mask_ref[...]], axis=1))
            return lax.dot_general(
                jnp.concatenate(left, axis=0),
                keys_ref[...],
                (((1,), (1,)), ((), ())),
                preferred_element_type=jnp.float32,
            )

        scores = scores_of(0)
        for n in blocks:
            following = scores_of(n + 1) if n + 1 < len(blocks) else None
            largest = jnp.max(scores, axis=1, keepdims=True)
            weights = jnp.exp2((scores - largest) * factor)
            summed = jnp.sum(weights, axis=1, keepdims=True)
            mixed = jnp.dot(
                weights.astype(jnp.bfloat16), values_ref[...], preferred_element_type=jnp.float32
            )
            mixed = mixed / jnp.maximum(summed, 1.0)
            for j in range(stack):
                one = jnp.where(some, mixed[j * rows : (j + 1) * rows], 0.0)
                at = (n * stack + j) * head_dim
                result_ref[:, at : at + head_dim] = one.astype(jnp.bfloat16)
            scores = following
        store = pltpu.make_async_copy(result_ref, out_ref.at[:, pl.ds(column, block_width)], sem)
        store.start()
        store.wait()

    operands = [queries, row_mask, token_bias]
    for source in sources:
        operands += source
    in_specs = [VMEM] * len(operands)
    aliases = {}
    if previous is not None:
        aliases = {len(operands): 0}
        operands.append(previous)
        in_specs.append(ANYWHERE)
    return pl.pallas_call(
        kernel,
        in_specs=in_specs,
        out_specs=ANYWHERE,
        out_shape=jax.ShapeDtypeStruct((rows, width), jnp.bfloat16),
        scratch_shapes=[
            pltpu.VMEM((tokens, 2 * head_dim), jnp.bfloat16),
            pltpu.VMEM((tokens, head_dim), jnp.bfloat16),
            pltpu.VMEM((rows, block_width), jnp.bfloat16),
            pltpu.SemaphoreType.DMA,
        ],
        input_output_aliases=aliases,
        compiler_params=params(16),
        cost_estimate=pl.CostEstimate(
            flops=6 * rows * group * tokens * head_dim,
            bytes_accessed=rows * block_width * 4,
            transcendentals=rows * group * tokens,
        ),
        name="attend",
    )(*operands)


def shards(queries, vis_feats, kv_weight, key_gain, cross_mask, image_tokens, image_owner):
    head_count = lax.axis_size("head")
    ctx_count = lax.axis_size("ctx")
    ctx_bits = ctx_count.bit_length() - 1
    head_dim = key_gain.shape[0]
    kv_heads = kv_weight.shape[1] // (2 * head_dim)
    per_kv = head_count // kv_heads
    images = image_tokens.shape[0]

    masks = mask_columns(cross_mask, image_tokens, head_dim, queries.shape[0])
    partial_sums, (row_mask, token_bias) = sum_over_head(vis_feats, kv_weight, 2 * head_dim, masks)

    def spread(piece):
        block, other = finish_chunk(
            partial_sums[piece], key_gain, image_tokens, image_owner, per_kv, piece == 0
        )
        if per_kv > 1:
            groups = [[k * per_kv + j for j in range(per_kv)] for k in range(kv_heads)]
            block, other = lax.psum((block, other), "head", axis_index_groups=groups)
        block = block + swapped(other, "ctx", 0)
        for step in range(1, ctx_bits):
            pairs = [
                (c, c ^ (2**step if c % 2 == 0 else 2 ** (ctx_bits - step))) for c in range(ctx_count)
            ]
            block = block + lax.ppermute(block, "ctx", pairs)
        other = swapped(block, "ctx", 0)
        return jnp.concatenate([block, other], 0)

    keys, values = spread(0), spread(1)

    if per_kv > 1:
        groups = [[k * per_kv + j for k in range(kv_heads)] for j in range(per_kv)]
        keys = lax.all_gather(keys, "head", axis_index_groups=groups)
        values = lax.all_gather(values, "head", axis_index_groups=groups)
        out = None
        for k in range(kv_heads):
            own = (keys[k], values[k])
            out = attend(0, own, [], queries, row_mask, token_bias, kv_heads, images, out, k)
        return out

    def place(c, h):
        return c * head_count + h

    own = (keys, values)
    arrivals = []
    out = attend(0, own, arrivals, queries, row_mask, token_bias, kv_heads, images, None)
    passing = [keys, values]
    for hop in range(1, head_count):
        pairs = []
        for c in range(ctx_count):
            for i in range(hop - 1, head_count - 1):
                if c % 2 == 0:
                    pairs.append((place(c, i), place(c, i + 1)))
                else:
                    pairs.append((place(c, head_count - 1 - i), place(c, head_count - 2 - i)))
        crossing = [None, None]
        for piece in range(2):
            passing[piece] = lax.ppermute(passing[piece], ("ctx", "head"), pairs)
            crossing[piece] = swapped(passing[piece], "ctx", 0)
        arrivals.append([tuple(passing), tuple(crossing)])
        out = attend(hop, own, arrivals, queries, row_mask, token_bias, kv_heads, images, out)
    return out


def solution(mesh):
    return jax.shard_map(
        shards,
        mesh=mesh,
        in_specs=(
            P(("ctx", "head"), None),
            P("ctx", "head"),
            P("head", None),
            P(),
            P("ctx", None),
            P(),
            P(),
        ),
        out_specs=P(("ctx", "head"), None),
        check_vma=False,
    )
```

```python
import math

import jax
import jax.numpy as jnp
from jax import lax
from jax.experimental import pallas as pl
from jax.experimental.pallas import tpu as pltpu
from jax.sharding import PartitionSpec as P

EPSILON = 1e-05
FLOOR_SCORE = -1e30
KV_TOTAL = 1280
STACK = 2
MIB = 2**20
EDGES = [(0, 1), (1, 0), (2, 3), (3, 2)]
MIDDLE = [(1, 2), (2, 1)]
OUTWARD = [(1, 0), (2, 3)]

VMEM = pl.BlockSpec(memory_space=pltpu.VMEM)
SMEM = pl.BlockSpec(memory_space=pltpu.SMEM)
ANYWHERE = pl.BlockSpec(memory_space=pl.ANY)
HBM = pl.BlockSpec(memory_space=pltpu.HBM)


def params(mib):
    return pltpu.CompilerParams(vmem_limit_bytes=mib * MIB)


def swapped(value, axis, bit):
    mask = 2**bit
    pairs = [(source, source ^ mask) for source in range(lax.axis_size(axis))]
    return lax.ppermute(value, axis, pairs)


def project(chunk_of, wanted, vis_feats, kv_weight, pair):
    count = lax.axis_size("head")
    rows, width = vis_feats.shape
    per_kv = count // (kv_weight.shape[1] // pair)
    block_rows = rows // per_kv
    head_dim = pair // 2
    alone = wanted == 1
    steps = 4
    few, deep = rows // steps, width // steps

    def kernel(feats_ref, weight_ref, *refs):
        out_refs = refs[: 2 * wanted]
        chunks = [chunk_of(lax.axis_index("head"), n) for n in range(wanted)]
        columns = [pl.multiple_of((chunk // per_kv) * pair, pair) for chunk in chunks]
        if alone:
            feats_vmem, weight_vmem, sems = refs[2 * wanted :]
            copies = []
            for n in range(steps):
                span = pl.ds(n * few, few)
                copies.append((feats_ref.at[span], feats_vmem.at[span], sems.at[n]))
            for n in range(steps):
                span = pl.ds(n * deep, deep)
                source = weight_ref.at[span, pl.ds(columns[0], pair)]
                copies.append((source, weight_vmem.at[span], sems.at[steps + n]))
            copies = [pltpu.make_async_copy(*copy) for copy in copies]
            for copy in copies:
                copy.start()
            for copy in copies:
                copy.wait()
            feats_ref, weight_ref, columns = feats_vmem, weight_vmem, [0]
        for n in range(wanted):
            row = 0 if per_kv == 1 else pl.multiple_of((chunks[n] % per_kv) * block_rows, block_rows)
            out = jnp.dot(
                feats_ref[pl.ds(row, block_rows), :],
                weight_ref[:, pl.ds(columns[n], pair)],
                preferred_element_type=jnp.float32,
            )
            out_refs[2 * n][...] = out[:, :head_dim]
            out_refs[2 * n + 1][...] = out[:, head_dim:]

    scratch = [
        pltpu.VMEM((rows, width), vis_feats.dtype),
        pltpu.VMEM((width, pair), kv_weight.dtype),
        pltpu.SemaphoreType.DMA((2 * steps,)),
    ]
    if alone:
        vis_feats = pltpu.with_memory_space_constraint(vis_feats, pltpu.HBM)
        kv_weight = pltpu.with_memory_space_constraint(kv_weight, pltpu.HBM)
    flat = pl.pallas_call(
        kernel,
        in_specs=[HBM, HBM] if alone else [VMEM, VMEM],
        out_specs=[VMEM] * (2 * wanted),
        out_shape=[jax.ShapeDtypeStruct((block_rows, head_dim), jnp.float32)] * (2 * wanted),
        scratch_shapes=scratch if alone else [],
        compiler_params=params(10),
        cost_estimate=pl.CostEstimate(
            flops=2 * wanted * block_rows * width * pair,
            bytes_accessed=(wanted * pair + rows) * width * 2,
            transcendentals=0,
        ),
        name="project",
    )(vis_feats, kv_weight)
    return [flat[2 * n : 2 * n + 2] for n in range(wanted)]


def sum_over_head(vis_feats, kv_weight, pair, early):
    count = lax.axis_size("head")
    ends = project(lambda here, n: count - 1 - here, 1, vis_feats, kv_weight, pair)[0]
    offsets = []
    for hop in range(2, count):
        offsets += [o for o in dict.fromkeys((count - hop, hop)) if o not in offsets]
    offsets.append(0)

    def rest(here, n):
        chunk = here + offsets[n]
        return jnp.where(chunk >= count, chunk - count, chunk)

    parts = dict(zip(offsets, project(rest, len(offsets), vis_feats, kv_weight, pair)))
    held = lax.optimization_barrier((ends[1], parts[0][0], *early))
    ends = (ends[0], held[0])
    parts[0] = (held[1], parts[0][1])
    early = held[2:]

    to_right, to_left = [None] * 2, [None] * 2
    for hop in range(1, count):
        senders = range(min(hop, count - 1))
        right_pairs = [(i, i + 1) for i in senders]
        left_pairs = [(count - 1 - i, count - 2 - i) for i in senders]
        for piece in range(2):
            if hop == 1 and count > 3:
                arrived = lax.ppermute(ends[piece], "head", right_pairs + left_pairs)
                to_right[piece] = to_left[piece] = arrived
                continue
            if hop == 1:
                right = left = ends[piece]
            elif hop == 2 and count == 4:
                right = left = parts[2][piece] + to_right[piece]
            else:
                right = parts[count - hop][piece] + to_right[piece]
                left = parts[hop][piece] + to_left[piece]
            to_right[piece] = lax.ppermute(right, "head", right_pairs)
            to_left[piece] = lax.ppermute(left, "head", left_pairs)
    return [[parts[0][piece], to_right[piece], to_left[piece]] for piece in range(2)], early


def swap_sums(vis_feats, kv_weight, pair, early):
    def first(here, n):
        return jnp.where(here < 2, 3, 0)

    def later(here, n):
        return (jnp.where(here < 2, 2, 1), jnp.where(here < 2, 1 - here, 5 - here), here)[n]

    far = project(first, 1, vis_feats, kv_weight, pair)[0]
    near, last, own = project(later, 3, vis_feats, kv_weight, pair)
    held = lax.optimization_barrier((far[1], own[0], *early))
    far, own, early = (far[0], held[0]), (held[1], own[1]), held[2:]

    def swap(value, pairs):
        return lax.ppermute(value, "head", pairs)

    def add(left, right):
        return left + right

    sums = []
    for piece in range(2):
        for_far = swap(far[piece], EDGES)
        for_near = swap(near[piece], EDGES)
        for_far = swap(add(far[piece], for_far), MIDDLE)
        for_near = swap(add(near[piece], for_near), MIDDLE)
        final = swap(add(last[piece], for_far), EDGES)
        sums.append([own[piece], final, for_near])
    return sums, early


def finish_chunk(partial_sums, key_gain, image_tokens, image_owner, per_kv, are_keys):
    rows, head_dim = partial_sums[0].shape
    half = KV_TOTAL // 2
    images = image_owner.shape[0]

    def kernel(tokens_ref, owner_ref, own_ref, left_ref, right_ref, gain_ref, mine_ref, other_ref):
        data = own_ref[...] + left_ref[...] + right_ref[...]
        if are_keys:
            mean = jnp.mean(data * data, axis=-1, keepdims=True)
            data = data * lax.rsqrt(mean + EPSILON) * gain_ref[...]
        data = data.astype(jnp.bfloat16)
        ctx = lax.axis_index("ctx")
        start, count, before = jnp.int32(0), jnp.int32(0), jnp.int32(0)
        for i in range(images):
            here = owner_ref[i] == ctx
            start = jnp.where(here, before, start)
            count = jnp.where(here, tokens_ref[i], count)
            before = before + tokens_ref[i]
        token = lax.broadcasted_iota(jnp.int32, (half, rows), 1) + (lax.axis_index("head") % per_kv) * rows
        token = jnp.where(token < count, token, -2 * KV_TOTAL)
        row = lax.broadcasted_iota(jnp.int32, (half, rows), 0)
        core = ctx % 2
        for ref, side in ((other_ref, 1 - core), (mine_ref, core)):
            match = (row + (side * half - start)) == token
            chosen = jnp.where(match, 1.0, 0.0).astype(jnp.bfloat16)
            ref[...] = jnp.dot(chosen, data, preferred_element_type=jnp.float32).astype(jnp.bfloat16)

    return pl.pallas_call(
        kernel,
        in_specs=[SMEM] * 2 + [VMEM] * 4,
        out_specs=[VMEM] * 2,
        out_shape=[jax.ShapeDtypeStruct((half, head_dim), jnp.bfloat16)] * 2,
        compiler_params=params(16),
        cost_estimate=pl.CostEstimate(
            flops=4 * half * rows * head_dim, bytes_accessed=12 * rows * head_dim, transcendentals=0
        ),
        name="finish",
    )(image_tokens, image_owner, *partial_sums, key_gain[None, :])


def mask_columns(cross_mask, image_tokens, head_dim, rows):
    images = image_tokens.shape[0]

    def kernel(tokens_ref, cross_ref, row_ref, bias_ref):
        here = pl.multiple_of(lax.axis_index("head") * rows, rows)
        cross = cross_ref[pl.ds(here, rows), :].astype(jnp.float32)
        column = lax.broadcasted_iota(jnp.int32, row_ref.shape, 1)
        closed = jnp.ones(row_ref.shape, jnp.float32)
        for i in range(images):
            closed = jnp.where(column == i, 1.0 - cross[:, i : i + 1], closed)
        row_ref[...] = closed.astype(jnp.bfloat16)
        row = lax.broadcasted_iota(jnp.int32, bias_ref.shape, 0)
        column = lax.broadcasted_iota(jnp.int32, bias_ref.shape, 1)
        before = jnp.int32(0)
        bias = jnp.zeros(bias_ref.shape, jnp.float32)
        for i in range(images + 1):
            after = before + tokens_ref[i] if i < images else jnp.int32(KV_TOTAL)
            inside = (column == i) & (row >= before) & (row < after)
            bias = jnp.where(inside, FLOOR_SCORE, bias)
            before = after
        bias_ref[...] = bias.astype(jnp.bfloat16)

    return pl.pallas_call(
        kernel,
        in_specs=[SMEM, VMEM],
        out_specs=[VMEM] * 2,
        out_shape=[
            jax.ShapeDtypeStruct((rows, head_dim), jnp.bfloat16),
            jax.ShapeDtypeStruct((KV_TOTAL, head_dim), jnp.bfloat16),
        ],
        compiler_params=params(8),
        name="masks",
    )(image_tokens, cross_mask)


def put_halves(mine_ref, other_ref, first, put):
    half = KV_TOTAL // 2
    core = lax.axis_index("ctx") % 2
    for at, ref in ((core, mine_ref), (1 - core, other_ref)):
        put(pl.ds(pl.multiple_of(at * half, half), half), ref[first : first + half, :])


def attend(head_of, first, keys, values, queries, row_mask, token_bias, kv_heads, images):
    rows, width = queries.shape
    tokens, head_dim = KV_TOTAL, keys[0].shape[1]
    block_width = width // kv_heads
    group = block_width // head_dim
    factor = head_dim ** (-0.5) * math.log2(math.e)
    stack = min(STACK, group)
    blocks = range(group // stack)
    whole = values is not None

    def kernel(*refs):
        queries_ref, mask_ref, bias_ref, *key_refs = refs[:5]
        if whole:
            *value_refs, result_ref, keys_ref, values_ref = refs[5:]

            def put_values(span, half):
                values_ref[span, :] = half

            put_halves(*value_refs, first, put_values)
        else:
            weights_ref, sums_ref, keys_ref = refs[5:]

        def put_keys(span, half):
            keys_ref[span, :head_dim] = half

        put_halves(*key_refs, first, put_keys)
        keys_ref[:, head_dim:] = bias_ref[...]
        column = pl.multiple_of(head_of(lax.axis_index("head")) * block_width, block_width)
        some = jnp.min(mask_ref[:, :images].astype(jnp.float32), axis=1, keepdims=True) < 0.5

        def scores_of(n):
            left = []
            for j in range(n * stack, (n + 1) * stack):
                query = queries_ref[:, pl.ds(column + j * head_dim, head_dim)]
                left.append(jnp.concatenate([query, mask_ref[...]], axis=1))
            return lax.dot_general(
                jnp.concatenate(left, axis=0),
                keys_ref[...],
                (((1,), (1,)), ((), ())),
                preferred_element_type=jnp.float32,
            )

        scores = scores_of(0)
        for n in blocks:
            following = scores_of(n + 1) if n + 1 < len(blocks) else None
            largest = jnp.max(scores, axis=1, keepdims=True)
            weights = jnp.exp2((scores - largest) * factor)
            summed = jnp.maximum(jnp.sum(weights, axis=1, keepdims=True), 1.0)
            weights = weights.astype(jnp.bfloat16)
            scores = following
            if not whole:
                span = slice(n * stack * rows, (n + 1) * stack * rows)
                weights_ref[span, :] = weights
                sums_ref[span, :] = jnp.broadcast_to(summed, (stack * rows, head_dim))
                continue
            mixed = jnp.dot(weights, values_ref[...], preferred_element_type=jnp.float32) / summed
            for j in range(stack):
                one = jnp.where(some, mixed[j * rows : (j + 1) * rows], 0.0)
                at = (n * stack + j) * head_dim
                result_ref[:, at : at + head_dim] = one.astype(jnp.bfloat16)

    operands = [queries, row_mask, token_bias, *keys, *(values or ())]
    if whole:
        out_shape = [jax.ShapeDtypeStruct((rows, block_width), jnp.bfloat16)]
    else:
        out_shape = [
            jax.ShapeDtypeStruct((group * rows, tokens), jnp.bfloat16),
            jax.ShapeDtypeStruct((group * rows, head_dim), jnp.float32),
        ]
    scratch = [pltpu.VMEM((tokens, 2 * head_dim), jnp.bfloat16)]
    if whole:
        scratch.append(pltpu.VMEM((tokens, head_dim), jnp.bfloat16))
    return pl.pallas_call(
        kernel,
        in_specs=[VMEM] * len(operands),
        out_specs=[VMEM] * len(out_shape),
        out_shape=out_shape,
        scratch_shapes=scratch,
        compiler_params=params(14),
        cost_estimate=pl.CostEstimate(
            flops=(6 if whole else 4) * rows * group * tokens * head_dim,
            bytes_accessed=rows * block_width * 2,
            transcendentals=rows * group * tokens,
        ),
        name="attend" if whole else "weigh",
    )(*operands)


def mix_far(heads_of, values, weighed, row_mask, earlier, images):
    head_dim = values[0].shape[1]
    rows = row_mask.shape[0]
    block_width = earlier[0].shape[1]
    group = block_width // head_dim
    before, count = len(earlier), len(weighed)
    half = KV_TOTAL // 2

    def kernel(*refs):
        weighed_refs, refs = refs[: 2 * count], refs[2 * count :]
        mask_ref, mine_ref, other_ref = refs[:3]
        earlier_refs = refs[3 : 3 + before]
        out_ref, values_ref, result_ref, sems = refs[3 + before :]
        here = lax.axis_index("head")

        def store(n, ref):
            column = pl.multiple_of(heads_of[n](here) * block_width, block_width)
            return pltpu.make_async_copy(ref, out_ref.at[:, pl.ds(column, block_width)], sems.at[n])

        for n, ref in enumerate(earlier_refs):
            store(n, ref).start()
        some = jnp.min(mask_ref[:, :images].astype(jnp.float32), axis=1, keepdims=True) < 0.5
        for n in range(count):

            def put(span, block):
                values_ref[n, span, :] = block

            put_halves(mine_ref, other_ref, n * half, put)
        for n in range(count):
            mixed = jnp.dot(weighed_refs[2 * n][...], values_ref[n], preferred_element_type=jnp.float32)
            mixed = mixed / weighed_refs[2 * n + 1][...]
            for j in range(group):
                one = jnp.where(some, mixed[j * rows : (j + 1) * rows], 0.0)
                result_ref[n, :, j * head_dim : (j + 1) * head_dim] = one.astype(jnp.bfloat16)
            store(before + n, result_ref.at[n]).start()
        for n, ref in enumerate(earlier_refs):
            store(n, ref).wait()
        for n in range(count):
            store(before + n, result_ref.at[n]).wait()

    operands = [array for pair in weighed for array in pair] + [row_mask, *values, *earlier]
    return pl.pallas_call(
        kernel,
        in_specs=[VMEM] * len(operands),
        out_specs=HBM,
        out_shape=jax.ShapeDtypeStruct((rows, (before + count) * block_width), jnp.bfloat16),
        scratch_shapes=[
            pltpu.VMEM((count, KV_TOTAL, head_dim), jnp.bfloat16),
            pltpu.VMEM((count, rows, block_width), jnp.bfloat16),
            pltpu.SemaphoreType.DMA((before + count,)),
        ],
        compiler_params=params(12),
        cost_estimate=pl.CostEstimate(
            flops=2 * count * rows * group * KV_TOTAL * head_dim,
            bytes_accessed=rows * block_width * 2 * (before + count),
            transcendentals=0,
        ),
        name="mix_far",
    )(*operands)


def shards(queries, vis_feats, kv_weight, key_gain, cross_mask, image_tokens, image_owner):
    head_count = lax.axis_size("head")
    ctx_count = lax.axis_size("ctx")
    ctx_bits = ctx_count.bit_length() - 1
    head_dim = key_gain.shape[0]
    kv_heads = kv_weight.shape[1] // (2 * head_dim)
    per_kv = head_count // kv_heads
    images = image_tokens.shape[0]

    masks = mask_columns(cross_mask, image_tokens, head_dim, queries.shape[0])
    add_up = swap_sums if head_count == 4 else sum_over_head
    partial_sums, (row_mask, token_bias) = add_up(vis_feats, kv_weight, 2 * head_dim, masks)

    def spread(piece):
        block, other = finish_chunk(
            partial_sums[piece], key_gain, image_tokens, image_owner, per_kv, piece == 0
        )
        if per_kv > 1:
            groups = [[k * per_kv + j for j in range(per_kv)] for k in range(kv_heads)]
            block, other = lax.psum((block, other), "head", axis_index_groups=groups)
        block = block + swapped(other, "ctx", 0)
        for step in range(1, ctx_bits):
            pairs = [
                (c, c ^ (2**step if c % 2 == 0 else 2 ** (ctx_bits - step))) for c in range(ctx_count)
            ]
            block = block + lax.ppermute(block, "ctx", pairs)
        return block

    keys, values = spread(0), spread(1)

    def run(head_of, first, keys, values):
        return attend(head_of, first, keys, values, queries, row_mask, token_bias, kv_heads, images)

    def join(block):
        return block, swapped(block, "ctx", 0)

    if head_count != 4 or per_kv > 1:
        groups = [[k * per_kv + j for k in range(kv_heads)] for j in range(per_kv)]
        keys, values = (
            join(lax.all_gather(block, "head", axis_index_groups=groups))
            for block in (keys, values)
        )
        parts = []
        for k in range(kv_heads):
            halves = ([mine[k], other[k]] for mine, other in (keys, values))
            parts += run(lambda here, k=k: k, 0, *halves)
        return jnp.concatenate(parts, axis=1)

    held = [[], [], [], []]
    for block in (keys, values):

        def swap(value, pairs):
            return lax.ppermute(value, "head", pairs)

        near = swap(block, EDGES)
        inner = swap(block, MIDDLE)
        outer = swap(near, MIDDLE)
        inner = inner + swap(inner, OUTWARD)
        outer = outer + swap(outer, OUTWARD)
        for n, half in enumerate((block, near, inner, outer)):
            held[n].append(join(half))
    heads_of = [
        lambda here: here,
        lambda here: jnp.where(here % 2 == 0, here + 1, here - 1),
        lambda here: jnp.where(here < 2, 2, 1),
        lambda here: jnp.where(here < 2, 3, 0),
    ]
    parts = []
    for n in range(3):
        parts += run(heads_of[n], 0, *held[n])
    weighed = [run(heads_of[3], 0, held[3][0], None)]
    return mix_far(heads_of, held[3][1], weighed, row_mask, parts, images)


def solution(mesh):
    return jax.shard_map(
        shards,
        mesh=mesh,
        in_specs=(
            P(("ctx", "head"), None),
            P("ctx", "head"),
            P("head", None),
            P(),
            P("ctx", None),
            P(),
            P(),
        ),
        out_specs=P(("ctx", "head"), None),
        check_vma=False,
    )
```

```python
import math

import jax
import jax.numpy as jnp
from jax import lax
from jax.experimental import pallas as pl
from jax.experimental.pallas import tpu as pltpu
from jax.sharding import PartitionSpec as P

EPSILON = 1e-05
FLOOR_SCORE = -1e30
KV_TOTAL = 1280
STACK = 2
MIB = 2**20
EDGES = [(0, 1), (1, 0), (2, 3), (3, 2)]
MIDDLE = [(1, 2), (2, 1)]
OUTWARD = [(1, 0), (2, 3)]

VMEM = pl.BlockSpec(memory_space=pltpu.VMEM)
SMEM = pl.BlockSpec(memory_space=pltpu.SMEM)
ANYWHERE = pl.BlockSpec(memory_space=pl.ANY)
HBM = pl.BlockSpec(memory_space=pltpu.HBM)


def params(mib):
    return pltpu.CompilerParams(vmem_limit_bytes=mib * MIB)


def swapped(value, axis, bit):
    mask = 2**bit
    pairs = [(source, source ^ mask) for source in range(lax.axis_size(axis))]
    return lax.ppermute(value, axis, pairs)


def project(chunk_of, wanted, vis_feats, kv_weight, pair):
    count = lax.axis_size("head")
    rows, width = vis_feats.shape
    per_kv = count // (kv_weight.shape[1] // pair)
    block_rows = rows // per_kv
    head_dim = pair // 2
    alone = wanted == 1
    steps = 4
    few, deep = rows // steps, width // steps

    def kernel(feats_ref, weight_ref, *refs):
        out_refs = refs[: 2 * wanted]
        chunks = [chunk_of(lax.axis_index("head"), n) for n in range(wanted)]
        columns = [pl.multiple_of((chunk // per_kv) * pair, pair) for chunk in chunks]
        if alone:
            feats_vmem, weight_vmem, sems = refs[2 * wanted :]
            copies = []
            for n in range(steps):
                span = pl.ds(n * few, few)
                copies.append((feats_ref.at[span], feats_vmem.at[span], sems.at[n]))
            for n in range(steps):
                span = pl.ds(n * deep, deep)
                source = weight_ref.at[span, pl.ds(columns[0], pair)]
                copies.append((source, weight_vmem.at[span], sems.at[steps + n]))
            copies = [pltpu.make_async_copy(*copy) for copy in copies]
            for copy in copies:
                copy.start()
            for copy in copies:
                copy.wait()
            feats_ref, weight_ref, columns = feats_vmem, weight_vmem, [0]
        for n in range(wanted):
            row = 0 if per_kv == 1 else pl.multiple_of((chunks[n] % per_kv) * block_rows, block_rows)
            out = jnp.dot(
                feats_ref[pl.ds(row, block_rows), :],
                weight_ref[:, pl.ds(columns[n], pair)],
                preferred_element_type=jnp.float32,
            )
            out_refs[2 * n][...] = out[:, :head_dim]
            out_refs[2 * n + 1][...] = out[:, head_dim:]

    scratch = [
        pltpu.VMEM((rows, width), vis_feats.dtype),
        pltpu.VMEM((width, pair), kv_weight.dtype),
        pltpu.SemaphoreType.DMA((2 * steps,)),
    ]
    if alone:
        vis_feats = pltpu.with_memory_space_constraint(vis_feats, pltpu.HBM)
        kv_weight = pltpu.with_memory_space_constraint(kv_weight, pltpu.HBM)
    flat = pl.pallas_call(
        kernel,
        in_specs=[HBM, HBM] if alone else [VMEM, VMEM],
        out_specs=[VMEM] * (2 * wanted),
        out_shape=[jax.ShapeDtypeStruct((block_rows, head_dim), jnp.float32)] * (2 * wanted),
        scratch_shapes=scratch if alone else [],
        compiler_params=params(10),
        cost_estimate=pl.CostEstimate(
            flops=2 * wanted * block_rows * width * pair,
            bytes_accessed=(wanted * pair + rows) * width * 2,
            transcendentals=0,
        ),
        name="project",
    )(vis_feats, kv_weight)
    return [flat[2 * n : 2 * n + 2] for n in range(wanted)]


def sum_over_head(vis_feats, kv_weight, pair, early):
    count = lax.axis_size("head")
    ends = project(lambda here, n: count - 1 - here, 1, vis_feats, kv_weight, pair)[0]
    offsets = []
    for hop in range(2, count):
        offsets += [o for o in dict.fromkeys((count - hop, hop)) if o not in offsets]
    offsets.append(0)

    def rest(here, n):
        chunk = here + offsets[n]
        return jnp.where(chunk >= count, chunk - count, chunk)

    parts = dict(zip(offsets, project(rest, len(offsets), vis_feats, kv_weight, pair)))
    held = lax.optimization_barrier((ends[1], parts[0][0], *early))
    ends = (ends[0], held[0])
    parts[0] = (held[1], parts[0][1])
    early = held[2:]

    to_right, to_left = [None] * 2, [None] * 2
    for hop in range(1, count):
        senders = range(min(hop, count - 1))
        right_pairs = [(i, i + 1) for i in senders]
        left_pairs = [(count - 1 - i, count - 2 - i) for i in senders]
        for piece in range(2):
            if hop == 1 and count > 3:
                arrived = lax.ppermute(ends[piece], "head", right_pairs + left_pairs)
                to_right[piece] = to_left[piece] = arrived
                continue
            if hop == 1:
                right = left = ends[piece]
            elif hop == 2 and count == 4:
                right = left = parts[2][piece] + to_right[piece]
            else:
                right = parts[count - hop][piece] + to_right[piece]
                left = parts[hop][piece] + to_left[piece]
            to_right[piece] = lax.ppermute(right, "head", right_pairs)
            to_left[piece] = lax.ppermute(left, "head", left_pairs)
    return [[parts[0][piece], to_right[piece], to_left[piece]] for piece in range(2)], early


def swap_middle(value):
    pairs = []
    for c in range(lax.axis_size("ctx")):
        pairs += [((c, 1), (c, 2)), ((c, 2), (c, 1)), ((c, 0), (c ^ 1, 0)), ((c, 3), (c ^ 1, 3))]
    pairs = [tuple(c * 4 + h for c, h in pair) for pair in pairs]
    return lax.ppermute(value, ("ctx", "head"), pairs)


def in_middle():
    here = lax.axis_index("head")
    return (here == 1) | (here == 2)


def add_in_middle(left, right):
    def kernel(left_ref, right_ref, out_ref):
        @pl.when(in_middle())
        def _():
            out_ref[...] = left_ref[...] + right_ref[...]

        @pl.when(jnp.logical_not(in_middle()))
        def _():
            out_ref[...] = left_ref[...]

    return pl.pallas_call(
        kernel,
        in_specs=[VMEM] * 2,
        out_specs=VMEM,
        out_shape=jax.ShapeDtypeStruct(left.shape, left.dtype),
        compiler_params=params(4),
        name="add_in_middle",
    )(left, right)


def pick_by_place(middle, end):
    def kernel(middle_ref, end_ref, out_ref):
        @pl.when(in_middle())
        def _():
            out_ref[...] = middle_ref[...]

        @pl.when(jnp.logical_not(in_middle()))
        def _():
            out_ref[...] = end_ref[...]

    return pl.pallas_call(
        kernel,
        in_specs=[VMEM] * 2,
        out_specs=VMEM,
        out_shape=jax.ShapeDtypeStruct(middle.shape, middle.dtype),
        compiler_params=params(4),
        name="pick_by_place",
    )(middle, end)


def swap_sums(vis_feats, kv_weight, pair, early):
    def first(here, n):
        return jnp.where(here < 2, 3, 0)

    def later(here, n):
        return (jnp.where(here < 2, 2, 1), jnp.where(here < 2, 1 - here, 5 - here), here)[n]

    far = project(first, 1, vis_feats, kv_weight, pair)[0]
    near, last, own = project(later, 3, vis_feats, kv_weight, pair)
    held = lax.optimization_barrier((far[1], own[0], *early))
    far, own, early = (far[0], held[0]), (held[1], own[1]), held[2:]

    def swap(value, pairs):
        return swap_middle(value) if pairs is MIDDLE else lax.ppermute(value, "head", pairs)

    def add(left, right):
        return left + right

    sums = []
    for piece in range(2):
        for_far = swap(far[piece], EDGES)
        for_near = swap(near[piece], EDGES)
        for_far = swap(add(far[piece], for_far), MIDDLE)
        for_near = swap(add(near[piece], for_near), MIDDLE)
        for_far = add_in_middle(last[piece], for_far)
        final = swap(for_far, EDGES)
        sums.append([own[piece], final, for_near])
    return sums, early


def finish_chunk(partial_sums, key_gain, image_tokens, image_owner, per_kv, are_keys, by_swaps):
    rows, head_dim = partial_sums[0].shape
    half = KV_TOTAL // 2
    images = image_owner.shape[0]

    def kernel(tokens_ref, owner_ref, own_ref, left_ref, right_ref, gain_ref, mine_ref, other_ref):
        data = own_ref[...] + left_ref[...]
        last = right_ref[...]
        data = data + (jnp.where(in_middle(), last, 0.0) if by_swaps else last)
        if are_keys:
            mean = jnp.mean(data * data, axis=-1, keepdims=True)
            data = data * lax.rsqrt(mean + EPSILON) * gain_ref[...]
        data = data.astype(jnp.bfloat16)
        ctx = lax.axis_index("ctx")
        start, count, before = jnp.int32(0), jnp.int32(0), jnp.int32(0)
        for i in range(images):
            here = owner_ref[i] == ctx
            start = jnp.where(here, before, start)
            count = jnp.where(here, tokens_ref[i], count)
            before = before + tokens_ref[i]
        token = lax.broadcasted_iota(jnp.int32, (half, rows), 1) + (lax.axis_index("head") % per_kv) * rows
        token = jnp.where(token < count, token, -2 * KV_TOTAL)
        row = lax.broadcasted_iota(jnp.int32, (half, rows), 0)
        core = ctx % 2
        for ref, side in ((other_ref, 1 - core), (mine_ref, core)):
            match = (row + (side * half - start)) == token
            chosen = jnp.where(match, 1.0, 0.0).astype(jnp.bfloat16)
            ref[...] = jnp.dot(chosen, data, preferred_element_type=jnp.float32).astype(jnp.bfloat16)

    return pl.pallas_call(
        kernel,
        in_specs=[SMEM] * 2 + [VMEM] * 4,
        out_specs=[VMEM] * 2,
        out_shape=[jax.ShapeDtypeStruct((half, head_dim), jnp.bfloat16)] * 2,
        compiler_params=params(16),
        cost_estimate=pl.CostEstimate(
            flops=4 * half * rows * head_dim, bytes_accessed=12 * rows * head_dim, transcendentals=0
        ),
        name="finish",
    )(image_tokens, image_owner, *partial_sums, key_gain[None, :])


def mask_columns(cross_mask, image_tokens, head_dim, rows):
    images = image_tokens.shape[0]

    def kernel(tokens_ref, cross_ref, row_ref, bias_ref):
        here = pl.multiple_of(lax.axis_index("head") * rows, rows)
        cross = cross_ref[pl.ds(here, rows), :].astype(jnp.float32)
        column = lax.broadcasted_iota(jnp.int32, row_ref.shape, 1)
        closed = jnp.ones(row_ref.shape, jnp.float32)
        for i in range(images):
            closed = jnp.where(column == i, 1.0 - cross[:, i : i + 1], closed)
        row_ref[...] = closed.astype(jnp.bfloat16)
        row = lax.broadcasted_iota(jnp.int32, bias_ref.shape, 0)
        column = lax.broadcasted_iota(jnp.int32, bias_ref.shape, 1)
        before = jnp.int32(0)
        bias = jnp.zeros(bias_ref.shape, jnp.float32)
        for i in range(images + 1):
            after = before + tokens_ref[i] if i < images else jnp.int32(KV_TOTAL)
            inside = (column == i) & (row >= before) & (row < after)
            bias = jnp.where(inside, FLOOR_SCORE, bias)
            before = after
        bias_ref[...] = bias.astype(jnp.bfloat16)

    return pl.pallas_call(
        kernel,
        in_specs=[SMEM, VMEM],
        out_specs=[VMEM] * 2,
        out_shape=[
            jax.ShapeDtypeStruct((rows, head_dim), jnp.bfloat16),
            jax.ShapeDtypeStruct((KV_TOTAL, head_dim), jnp.bfloat16),
        ],
        compiler_params=params(8),
        name="masks",
    )(image_tokens, cross_mask)


def put_halves(mine_ref, other_ref, first, put):
    half = KV_TOTAL // 2
    core = lax.axis_index("ctx") % 2
    for at, ref in ((core, mine_ref), (1 - core, other_ref)):
        put(pl.ds(pl.multiple_of(at * half, half), half), ref[first : first + half, :])


def attend(head_of, first, keys, values, queries, row_mask, token_bias, kv_heads, images):
    rows, width = queries.shape
    tokens, head_dim = KV_TOTAL, keys[0].shape[1]
    block_width = width // kv_heads
    group = block_width // head_dim
    factor = head_dim ** (-0.5) * math.log2(math.e)
    stack = min(STACK, group)
    blocks = range(group // stack)
    whole = values is not None

    def kernel(*refs):
        queries_ref, mask_ref, bias_ref, *key_refs = refs[:5]
        if whole:
            *value_refs, result_ref, keys_ref, values_ref = refs[5:]

            def put_values(span, half):
                values_ref[span, :] = half

            put_halves(*value_refs, first, put_values)
        else:
            weights_ref, sums_ref, keys_ref = refs[5:]

        def put_keys(span, half):
            keys_ref[span, :head_dim] = half

        put_halves(*key_refs, first, put_keys)
        keys_ref[:, head_dim:] = bias_ref[...]
        column = pl.multiple_of(head_of(lax.axis_index("head")) * block_width, block_width)
        some = jnp.min(mask_ref[:, :images].astype(jnp.float32), axis=1, keepdims=True) < 0.5

        def scores_of(n):
            left = []
            for j in range(n * stack, (n + 1) * stack):
                query = queries_ref[:, pl.ds(column + j * head_dim, head_dim)]
                left.append(jnp.concatenate([query, mask_ref[...]], axis=1))
            return lax.dot_general(
                jnp.concatenate(left, axis=0),
                keys_ref[...],
                (((1,), (1,)), ((), ())),
                preferred_element_type=jnp.float32,
            )

        scores = scores_of(0)
        for n in blocks:
            following = scores_of(n + 1) if n + 1 < len(blocks) else None
            largest = jnp.max(scores, axis=1, keepdims=True)
            weights = jnp.exp2((scores - largest) * factor)
            summed = jnp.maximum(jnp.sum(weights, axis=1, keepdims=True), 1.0)
            weights = weights.astype(jnp.bfloat16)
            scores = following
            if not whole:
                span = slice(n * stack * rows, (n + 1) * stack * rows)
                weights_ref[span, :] = weights
                sums_ref[span, :] = jnp.broadcast_to(summed, (stack * rows, head_dim))
                continue
            mixed = jnp.dot(weights, values_ref[...], preferred_element_type=jnp.float32) / summed
            for j in range(stack):
                one = jnp.where(some, mixed[j * rows : (j + 1) * rows], 0.0)
                at = (n * stack + j) * head_dim
                result_ref[:, at : at + head_dim] = one.astype(jnp.bfloat16)

    operands = [queries, row_mask, token_bias, *keys, *(values or ())]
    if whole:
        out_shape = [jax.ShapeDtypeStruct((rows, block_width), jnp.bfloat16)]
    else:
        out_shape = [
            jax.ShapeDtypeStruct((group * rows, tokens), jnp.bfloat16),
            jax.ShapeDtypeStruct((group * rows, head_dim), jnp.float32),
        ]
    scratch = [pltpu.VMEM((tokens, 2 * head_dim), jnp.bfloat16)]
    if whole:
        scratch.append(pltpu.VMEM((tokens, head_dim), jnp.bfloat16))
    return pl.pallas_call(
        kernel,
        in_specs=[VMEM] * len(operands),
        out_specs=[VMEM] * len(out_shape),
        out_shape=out_shape,
        scratch_shapes=scratch,
        compiler_params=params(14),
        cost_estimate=pl.CostEstimate(
            flops=(6 if whole else 4) * rows * group * tokens * head_dim,
            bytes_accessed=rows * block_width * 2,
            transcendentals=rows * group * tokens,
        ),
        name="attend" if whole else "weigh",
    )(*operands)


def mix_far(heads_of, values, weighed, row_mask, earlier, images):
    head_dim = values[0].shape[1]
    rows = row_mask.shape[0]
    block_width = earlier[0].shape[1]
    group = block_width // head_dim
    before, count = len(earlier), len(weighed)
    half = KV_TOTAL // 2

    def kernel(*refs):
        weighed_refs, refs = refs[: 2 * count], refs[2 * count :]
        mask_ref, mine_ref, other_ref = refs[:3]
        earlier_refs = refs[3 : 3 + before]
        out_ref, values_ref, result_ref, sems = refs[3 + before :]
        here = lax.axis_index("head")

        def store(n, ref):
            column = pl.multiple_of(heads_of[n](here) * block_width, block_width)
            return pltpu.make_async_copy(ref, out_ref.at[:, pl.ds(column, block_width)], sems.at[n])

        for n, ref in enumerate(earlier_refs):
            store(n, ref).start()
        some = jnp.min(mask_ref[:, :images].astype(jnp.float32), axis=1, keepdims=True) < 0.5
        for n in range(count):

            def put(span, block):
                values_ref[n, span, :] = block

            put_halves(mine_ref, other_ref, n * half, put)
        for n in range(count):
            mixed = jnp.dot(weighed_refs[2 * n][...], values_ref[n], preferred_element_type=jnp.float32)
            mixed = mixed / weighed_refs[2 * n + 1][...]
            for j in range(group):
                one = jnp.where(some, mixed[j * rows : (j + 1) * rows], 0.0)
                result_ref[n, :, j * head_dim : (j + 1) * head_dim] = one.astype(jnp.bfloat16)
            store(before + n, result_ref.at[n]).start()
        for n, ref in enumerate(earlier_refs):
            store(n, ref).wait()
        for n in range(count):
            store(before + n, result_ref.at[n]).wait()

    operands = [array for pair in weighed for array in pair] + [row_mask, *values, *earlier]
    return pl.pallas_call(
        kernel,
        in_specs=[VMEM] * len(operands),
        out_specs=HBM,
        out_shape=jax.ShapeDtypeStruct((rows, (before + count) * block_width), jnp.bfloat16),
        scratch_shapes=[
            pltpu.VMEM((count, KV_TOTAL, head_dim), jnp.bfloat16),
            pltpu.VMEM((count, rows, block_width), jnp.bfloat16),
            pltpu.SemaphoreType.DMA((before + count,)),
        ],
        compiler_params=params(12),
        cost_estimate=pl.CostEstimate(
            flops=2 * count * rows * group * KV_TOTAL * head_dim,
            bytes_accessed=rows * block_width * 2 * (before + count),
            transcendentals=0,
        ),
        name="mix_far",
    )(*operands)


def shards(queries, vis_feats, kv_weight, key_gain, cross_mask, image_tokens, image_owner):
    head_count = lax.axis_size("head")
    ctx_count = lax.axis_size("ctx")
    ctx_bits = ctx_count.bit_length() - 1
    head_dim = key_gain.shape[0]
    kv_heads = kv_weight.shape[1] // (2 * head_dim)
    per_kv = head_count // kv_heads
    images = image_tokens.shape[0]

    masks = mask_columns(cross_mask, image_tokens, head_dim, queries.shape[0])
    add_up = swap_sums if head_count == 4 else sum_over_head
    partial_sums, (row_mask, token_bias) = add_up(vis_feats, kv_weight, 2 * head_dim, masks)

    def spread(piece):
        block, other = finish_chunk(
            partial_sums[piece], key_gain, image_tokens, image_owner, per_kv, piece == 0, head_count == 4
        )
        if per_kv > 1:
            groups = [[k * per_kv + j for j in range(per_kv)] for k in range(kv_heads)]
            block, other = lax.psum((block, other), "head", axis_index_groups=groups)
        block = block + swapped(other, "ctx", 0)
        for step in range(1, ctx_bits):
            pairs = [
                (c, c ^ (2**step if c % 2 == 0 else 2 ** (ctx_bits - step))) for c in range(ctx_count)
            ]
            block = block + lax.ppermute(block, "ctx", pairs)
        return block

    keys, values = spread(0), spread(1)

    def run(head_of, first, keys, values):
        return attend(head_of, first, keys, values, queries, row_mask, token_bias, kv_heads, images)

    def join(block):
        return block, swapped(block, "ctx", 0)

    if head_count != 4 or per_kv > 1:
        groups = [[k * per_kv + j for k in range(kv_heads)] for j in range(per_kv)]
        keys, values = (
            join(lax.all_gather(block, "head", axis_index_groups=groups))
            for block in (keys, values)
        )
        parts = []
        for k in range(kv_heads):
            halves = ([mine[k], other[k]] for mine, other in (keys, values))
            parts += run(lambda here, k=k: k, 0, *halves)
        return jnp.concatenate(parts, axis=1)

    held = [[], [], [], []]
    for block in (keys, values):

        def swap(value, pairs):
            return swap_middle(value) if pairs is MIDDLE else lax.ppermute(value, "head", pairs)

        near = swap(block, EDGES)
        inner = swap(block, MIDDLE)
        outer = swap(near, MIDDLE)
        inner = pick_by_place(inner, swap(inner, OUTWARD))
        outer = pick_by_place(outer, swap(outer, OUTWARD))
        for n, half in enumerate((block, near, inner, outer)):
            held[n].append(join(half))
    heads_of = [
        lambda here: here,
        lambda here: jnp.where(here % 2 == 0, here + 1, here - 1),
        lambda here: jnp.where(here < 2, 2, 1),
        lambda here: jnp.where(here < 2, 3, 0),
    ]
    parts = []
    for n in range(3):
        parts += run(heads_of[n], 0, *held[n])
    weighed = [run(heads_of[3], 0, held[3][0], None)]
    return mix_far(heads_of, held[3][1], weighed, row_mask, parts, images)


def solution(mesh):
    return jax.shard_map(
        shards,
        mesh=mesh,
        in_specs=(
            P(("ctx", "head"), None),
            P("ctx", "head"),
            P("head", None),
            P(),
            P("ctx", None),
            P(),
            P(),
        ),
        out_specs=P(("ctx", "head"), None),
        check_vma=False,
    )
```

```python
import math

import jax
import jax.numpy as jnp
from jax import lax
from jax.experimental import pallas as pl
from jax.experimental.pallas import tpu as pltpu
from jax.sharding import PartitionSpec as P

EPSILON = 1e-05
FLOOR_SCORE = -1e30
KV_TOTAL = 1280
STACK = 2
MIB = 2**20
EDGES = [(0, 1), (1, 0), (2, 3), (3, 2)]
MIDDLE = [(1, 2), (2, 1)]
OUTWARD = [(1, 0), (2, 3)]

VMEM = pl.BlockSpec(memory_space=pltpu.VMEM)
SMEM = pl.BlockSpec(memory_space=pltpu.SMEM)
ANYWHERE = pl.BlockSpec(memory_space=pl.ANY)
HBM = pl.BlockSpec(memory_space=pltpu.HBM)


def params(mib):
    return pltpu.CompilerParams(vmem_limit_bytes=mib * MIB)


def swapped(value, axis, bit):
    mask = 2**bit
    pairs = [(source, source ^ mask) for source in range(lax.axis_size(axis))]
    return lax.ppermute(value, axis, pairs)


def project(chunk_of, wanted, vis_feats, kv_weight, pair):
    count = lax.axis_size("head")
    rows, width = vis_feats.shape
    per_kv = count // (kv_weight.shape[1] // pair)
    block_rows = rows // per_kv
    head_dim = pair // 2
    alone = wanted == 1
    steps = 4
    few, deep = rows // steps, width // steps

    def kernel(feats_ref, weight_ref, *refs):
        out_refs = refs[: 2 * wanted]
        chunks = [chunk_of(lax.axis_index("head"), n) for n in range(wanted)]
        columns = [pl.multiple_of((chunk // per_kv) * pair, pair) for chunk in chunks]
        if alone:
            feats_vmem, weight_vmem, sems = refs[2 * wanted :]
            copies = []
            for n in range(steps):
                span = pl.ds(n * few, few)
                copies.append((feats_ref.at[span], feats_vmem.at[span], sems.at[n]))
            for n in range(steps):
                span = pl.ds(n * deep, deep)
                source = weight_ref.at[span, pl.ds(columns[0], pair)]
                copies.append((source, weight_vmem.at[span], sems.at[steps + n]))
            copies = [pltpu.make_async_copy(*copy) for copy in copies]
            for copy in copies:
                copy.start()
            for copy in copies:
                copy.wait()
            feats_ref, weight_ref, columns = feats_vmem, weight_vmem, [0]
        for n in range(wanted):
            row = 0 if per_kv == 1 else pl.multiple_of((chunks[n] % per_kv) * block_rows, block_rows)
            out = jnp.dot(
                feats_ref[pl.ds(row, block_rows), :],
                weight_ref[:, pl.ds(columns[n], pair)],
                preferred_element_type=jnp.float32,
            )
            out_refs[2 * n][...] = out[:, :head_dim]
            out_refs[2 * n + 1][...] = out[:, head_dim:]

    scratch = [
        pltpu.VMEM((rows, width), vis_feats.dtype),
        pltpu.VMEM((width, pair), kv_weight.dtype),
        pltpu.SemaphoreType.DMA((2 * steps,)),
    ]
    if alone:
        vis_feats = pltpu.with_memory_space_constraint(vis_feats, pltpu.HBM)
        kv_weight = pltpu.with_memory_space_constraint(kv_weight, pltpu.HBM)
    flat = pl.pallas_call(
        kernel,
        in_specs=[HBM, HBM] if alone else [VMEM, VMEM],
        out_specs=[VMEM] * (2 * wanted),
        out_shape=[jax.ShapeDtypeStruct((block_rows, head_dim), jnp.float32)] * (2 * wanted),
        scratch_shapes=scratch if alone else [],
        compiler_params=params(10),
        cost_estimate=pl.CostEstimate(
            flops=2 * wanted * block_rows * width * pair,
            bytes_accessed=(wanted * pair + rows) * width * 2,
            transcendentals=0,
        ),
        name="project",
    )(vis_feats, kv_weight)
    return [flat[2 * n : 2 * n + 2] for n in range(wanted)]


def sum_over_head(vis_feats, kv_weight, pair, early):
    count = lax.axis_size("head")
    ends = project(lambda here, n: count - 1 - here, 1, vis_feats, kv_weight, pair)[0]
    offsets = []
    for hop in range(2, count):
        offsets += [o for o in dict.fromkeys((count - hop, hop)) if o not in offsets]
    offsets.append(0)

    def rest(here, n):
        chunk = here + offsets[n]
        return jnp.where(chunk >= count, chunk - count, chunk)

    parts = dict(zip(offsets, project(rest, len(offsets), vis_feats, kv_weight, pair)))
    held = lax.optimization_barrier((ends[1], parts[0][0], *early))
    ends = (ends[0], held[0])
    parts[0] = (held[1], parts[0][1])
    early = held[2:]

    to_right, to_left = [None] * 2, [None] * 2
    for hop in range(1, count):
        senders = range(min(hop, count - 1))
        right_pairs = [(i, i + 1) for i in senders]
        left_pairs = [(count - 1 - i, count - 2 - i) for i in senders]
        for piece in range(2):
            if hop == 1 and count > 3:
                arrived = lax.ppermute(ends[piece], "head", right_pairs + left_pairs)
                to_right[piece] = to_left[piece] = arrived
                continue
            if hop == 1:
                right = left = ends[piece]
            elif hop == 2 and count == 4:
                right = left = parts[2][piece] + to_right[piece]
            else:
                right = parts[count - hop][piece] + to_right[piece]
                left = parts[hop][piece] + to_left[piece]
            to_right[piece] = lax.ppermute(right, "head", right_pairs)
            to_left[piece] = lax.ppermute(left, "head", left_pairs)
    return [[parts[0][piece], to_right[piece], to_left[piece]] for piece in range(2)], early


def swap_middle(value):
    pairs = []
    for c in range(lax.axis_size("ctx")):
        pairs += [((c, 1), (c, 2)), ((c, 2), (c, 1)), ((c, 0), (c ^ 1, 0)), ((c, 3), (c ^ 1, 3))]
    pairs = [tuple(c * 4 + h for c, h in pair) for pair in pairs]
    return lax.ppermute(value, ("ctx", "head"), pairs)


def in_middle():
    here = lax.axis_index("head")
    return (here == 1) | (here == 2)


def add_in_middle(left, right):
    def kernel(left_ref, right_ref, out_ref):
        @pl.when(in_middle())
        def _():
            out_ref[...] = left_ref[...] + right_ref[...]

        @pl.when(jnp.logical_not(in_middle()))
        def _():
            out_ref[...] = left_ref[...]

    return pl.pallas_call(
        kernel,
        in_specs=[VMEM] * 2,
        out_specs=VMEM,
        out_shape=jax.ShapeDtypeStruct(left.shape, left.dtype),
        compiler_params=params(4),
        name="add_in_middle",
    )(left, right)


def pick_by_place(middle, end):
    def kernel(middle_ref, end_ref, out_ref):
        @pl.when(in_middle())
        def _():
            out_ref[...] = middle_ref[...]

        @pl.when(jnp.logical_not(in_middle()))
        def _():
            out_ref[...] = end_ref[...]

    return pl.pallas_call(
        kernel,
        in_specs=[VMEM] * 2,
        out_specs=VMEM,
        out_shape=jax.ShapeDtypeStruct(middle.shape, middle.dtype),
        compiler_params=params(4),
        name="pick_by_place",
    )(middle, end)


def swap_sums(vis_feats, kv_weight, pair, early):
    def first(here, n):
        return jnp.where(here < 2, 3, 0)

    def later(here, n):
        return (jnp.where(here < 2, 2, 1), jnp.where(here < 2, 1 - here, 5 - here), here)[n]

    far = project(first, 1, vis_feats, kv_weight, pair)[0]
    near, last, own = project(later, 3, vis_feats, kv_weight, pair)
    held = lax.optimization_barrier((far[1], own[0]))
    far, own = (far[0], held[0]), (held[1], own[1])

    def swap(value, pairs):
        return swap_middle(value) if pairs is MIDDLE else lax.ppermute(value, "head", pairs)

    def add(left, right):
        return left + right

    sums = []
    for piece in range(2):
        for_far = swap(far[piece], EDGES)
        for_near = swap(near[piece], EDGES)
        if piece == 1:
            held = lax.optimization_barrier((for_near, *early))
            for_near, early = held[0], held[1:]
        for_far = swap(add(far[piece], for_far), MIDDLE)
        for_near = swap(add(near[piece], for_near), MIDDLE)
        for_far = add_in_middle(last[piece], for_far)
        final = swap(for_far, EDGES)
        sums.append([own[piece], final, for_near])
    return sums, early


def finish_chunk(partial_sums, key_gain, image_tokens, image_owner, per_kv, are_keys, by_swaps):
    rows, head_dim = partial_sums[0].shape
    half = KV_TOTAL // 2
    images = image_owner.shape[0]

    def kernel(tokens_ref, owner_ref, own_ref, left_ref, right_ref, gain_ref, mine_ref, other_ref):
        data = own_ref[...] + left_ref[...]
        last = right_ref[...]
        data = data + (jnp.where(in_middle(), last, 0.0) if by_swaps else last)
        if are_keys:
            mean = jnp.mean(data * data, axis=-1, keepdims=True)
            data = data * lax.rsqrt(mean + EPSILON) * gain_ref[...]
        data = data.astype(jnp.bfloat16)
        ctx = lax.axis_index("ctx")
        start, count, before = jnp.int32(0), jnp.int32(0), jnp.int32(0)
        for i in range(images):
            here = owner_ref[i] == ctx
            start = jnp.where(here, before, start)
            count = jnp.where(here, tokens_ref[i], count)
            before = before + tokens_ref[i]
        token = lax.broadcasted_iota(jnp.int32, (half, rows), 1) + (lax.axis_index("head") % per_kv) * rows
        token = jnp.where(token < count, token, -2 * KV_TOTAL)
        row = lax.broadcasted_iota(jnp.int32, (half, rows), 0)
        core = ctx % 2
        for ref, side in ((other_ref, 1 - core), (mine_ref, core)):
            match = (row + (side * half - start)) == token
            chosen = jnp.where(match, 1.0, 0.0).astype(jnp.bfloat16)
            ref[...] = jnp.dot(chosen, data, preferred_element_type=jnp.float32).astype(jnp.bfloat16)

    return pl.pallas_call(
        kernel,
        in_specs=[SMEM] * 2 + [VMEM] * 4,
        out_specs=[VMEM] * 2,
        out_shape=[jax.ShapeDtypeStruct((half, head_dim), jnp.bfloat16)] * 2,
        compiler_params=params(16),
        cost_estimate=pl.CostEstimate(
            flops=4 * half * rows * head_dim, bytes_accessed=12 * rows * head_dim, transcendentals=0
        ),
        name="finish",
    )(image_tokens, image_owner, *partial_sums, key_gain[None, :])


def mask_columns(cross_mask, image_tokens, head_dim, rows):
    images = image_tokens.shape[0]

    def kernel(tokens_ref, cross_ref, row_ref, bias_ref):
        here = pl.multiple_of(lax.axis_index("head") * rows, rows)
        cross = cross_ref[pl.ds(here, rows), :].astype(jnp.float32)
        column = lax.broadcasted_iota(jnp.int32, row_ref.shape, 1)
        closed = jnp.ones(row_ref.shape, jnp.float32)
        for i in range(images):
            closed = jnp.where(column == i, 1.0 - cross[:, i : i + 1], closed)
        row_ref[...] = closed.astype(jnp.bfloat16)
        row = lax.broadcasted_iota(jnp.int32, bias_ref.shape, 0)
        column = lax.broadcasted_iota(jnp.int32, bias_ref.shape, 1)
        before = jnp.int32(0)
        bias = jnp.zeros(bias_ref.shape, jnp.float32)
        for i in range(images + 1):
            after = before + tokens_ref[i] if i < images else jnp.int32(KV_TOTAL)
            inside = (column == i) & (row >= before) & (row < after)
            bias = jnp.where(inside, FLOOR_SCORE, bias)
            before = after
        bias_ref[...] = bias.astype(jnp.bfloat16)

    return pl.pallas_call(
        kernel,
        in_specs=[SMEM, VMEM],
        out_specs=[VMEM] * 2,
        out_shape=[
            jax.ShapeDtypeStruct((rows, head_dim), jnp.bfloat16),
            jax.ShapeDtypeStruct((KV_TOTAL, head_dim), jnp.bfloat16),
        ],
        compiler_params=params(8),
        name="masks",
    )(image_tokens, cross_mask)


def put_halves(mine_ref, other_ref, first, put):
    half = KV_TOTAL // 2
    core = lax.axis_index("ctx") % 2
    for at, ref in ((core, mine_ref), (1 - core, other_ref)):
        put(pl.ds(pl.multiple_of(at * half, half), half), ref[first : first + half, :])


def attend(head_of, first, keys, values, queries, row_mask, token_bias, kv_heads, images):
    rows, width = queries.shape
    tokens, head_dim = KV_TOTAL, keys[0].shape[1]
    block_width = width // kv_heads
    group = block_width // head_dim
    factor = head_dim ** (-0.5) * math.log2(math.e)
    stack = min(STACK, group)
    blocks = range(group // stack)
    whole = values is not None

    def kernel(*refs):
        queries_ref, mask_ref, bias_ref, *key_refs = refs[:5]
        if whole:
            *value_refs, result_ref, keys_ref, values_ref = refs[5:]

            def put_values(span, half):
                values_ref[span, :] = half

            put_halves(*value_refs, first, put_values)
        else:
            weights_ref, sums_ref, keys_ref = refs[5:]

        def put_keys(span, half):
            keys_ref[span, :head_dim] = half

        put_halves(*key_refs, first, put_keys)
        keys_ref[:, head_dim:] = bias_ref[...]
        column = pl.multiple_of(head_of(lax.axis_index("head")) * block_width, block_width)
        some = jnp.min(mask_ref[:, :images].astype(jnp.float32), axis=1, keepdims=True) < 0.5

        def scores_of(n):
            left = []
            for j in range(n * stack, (n + 1) * stack):
                query = queries_ref[:, pl.ds(column + j * head_dim, head_dim)]
                left.append(jnp.concatenate([query, mask_ref[...]], axis=1))
            return lax.dot_general(
                jnp.concatenate(left, axis=0),
                keys_ref[...],
                (((1,), (1,)), ((), ())),
                preferred_element_type=jnp.float32,
            )

        scores = scores_of(0)
        for n in blocks:
            following = scores_of(n + 1) if n + 1 < len(blocks) else None
            largest = jnp.max(scores, axis=1, keepdims=True)
            weights = jnp.exp2((scores - largest) * factor)
            summed = jnp.maximum(jnp.sum(weights, axis=1, keepdims=True), 1.0)
            weights = weights.astype(jnp.bfloat16)
            scores = following
            if not whole:
                span = slice(n * stack * rows, (n + 1) * stack * rows)
                weights_ref[span, :] = weights
                sums_ref[span, :] = jnp.broadcast_to(summed, (stack * rows, head_dim))
                continue
            mixed = jnp.dot(weights, values_ref[...], preferred_element_type=jnp.float32) / summed
            for j in range(stack):
                one = jnp.where(some, mixed[j * rows : (j + 1) * rows], 0.0)
                at = (n * stack + j) * head_dim
                result_ref[:, at : at + head_dim] = one.astype(jnp.bfloat16)

    operands = [queries, row_mask, token_bias, *keys, *(values or ())]
    if whole:
        out_shape = [jax.ShapeDtypeStruct((rows, block_width), jnp.bfloat16)]
    else:
        out_shape = [
            jax.ShapeDtypeStruct((group * rows, tokens), jnp.bfloat16),
            jax.ShapeDtypeStruct((group * rows, head_dim), jnp.float32),
        ]
    scratch = [pltpu.VMEM((tokens, 2 * head_dim), jnp.bfloat16)]
    if whole:
        scratch.append(pltpu.VMEM((tokens, head_dim), jnp.bfloat16))
    return pl.pallas_call(
        kernel,
        in_specs=[VMEM] * len(operands),
        out_specs=[VMEM] * len(out_shape),
        out_shape=out_shape,
        scratch_shapes=scratch,
        compiler_params=params(14),
        cost_estimate=pl.CostEstimate(
            flops=(6 if whole else 4) * rows * group * tokens * head_dim,
            bytes_accessed=rows * block_width * 2,
            transcendentals=rows * group * tokens,
        ),
        name="attend" if whole else "weigh",
    )(*operands)


def mix_far(heads_of, values, weighed, row_mask, earlier, images):
    head_dim = values[0].shape[1]
    rows = row_mask.shape[0]
    block_width = earlier[0].shape[1]
    group = block_width // head_dim
    before, count = len(earlier), len(weighed)
    half = KV_TOTAL // 2

    def kernel(*refs):
        weighed_refs, refs = refs[: 2 * count], refs[2 * count :]
        mask_ref, mine_ref, other_ref = refs[:3]
        earlier_refs = refs[3 : 3 + before]
        out_ref, values_ref, result_ref, sems = refs[3 + before :]
        here = lax.axis_index("head")

        def store(n, ref):
            column = pl.multiple_of(heads_of[n](here) * block_width, block_width)
            return pltpu.make_async_copy(ref, out_ref.at[:, pl.ds(column, block_width)], sems.at[n])

        for n, ref in enumerate(earlier_refs):
            store(n, ref).start()
        some = jnp.min(mask_ref[:, :images].astype(jnp.float32), axis=1, keepdims=True) < 0.5
        for n in range(count):

            def put(span, block):
                values_ref[n, span, :] = block

            put_halves(mine_ref, other_ref, n * half, put)
        for n in range(count):
            mixed = jnp.dot(weighed_refs[2 * n][...], values_ref[n], preferred_element_type=jnp.float32)
            mixed = mixed / weighed_refs[2 * n + 1][...]
            for j in range(group):
                one = jnp.where(some, mixed[j * rows : (j + 1) * rows], 0.0)
                result_ref[n, :, j * head_dim : (j + 1) * head_dim] = one.astype(jnp.bfloat16)
            store(before + n, result_ref.at[n]).start()
        for n, ref in enumerate(earlier_refs):
            store(n, ref).wait()
        for n in range(count):
            store(before + n, result_ref.at[n]).wait()

    operands = [array for pair in weighed for array in pair] + [row_mask, *values, *earlier]
    return pl.pallas_call(
        kernel,
        in_specs=[VMEM] * len(operands),
        out_specs=HBM,
        out_shape=jax.ShapeDtypeStruct((rows, (before + count) * block_width), jnp.bfloat16),
        scratch_shapes=[
            pltpu.VMEM((count, KV_TOTAL, head_dim), jnp.bfloat16),
            pltpu.VMEM((count, rows, block_width), jnp.bfloat16),
            pltpu.SemaphoreType.DMA((before + count,)),
        ],
        compiler_params=params(12),
        cost_estimate=pl.CostEstimate(
            flops=2 * count * rows * group * KV_TOTAL * head_dim,
            bytes_accessed=rows * block_width * 2 * (before + count),
            transcendentals=0,
        ),
        name="mix_far",
    )(*operands)


def shards(queries, vis_feats, kv_weight, key_gain, cross_mask, image_tokens, image_owner):
    head_count = lax.axis_size("head")
    ctx_count = lax.axis_size("ctx")
    ctx_bits = ctx_count.bit_length() - 1
    head_dim = key_gain.shape[0]
    kv_heads = kv_weight.shape[1] // (2 * head_dim)
    per_kv = head_count // kv_heads
    images = image_tokens.shape[0]

    masks = mask_columns(cross_mask, image_tokens, head_dim, queries.shape[0])
    add_up = swap_sums if head_count == 4 else sum_over_head
    partial_sums, (row_mask, token_bias) = add_up(vis_feats, kv_weight, 2 * head_dim, masks)

    def spread(piece):
        block, other = finish_chunk(
            partial_sums[piece], key_gain, image_tokens, image_owner, per_kv, piece == 0, head_count == 4
        )
        if per_kv > 1:
            groups = [[k * per_kv + j for j in range(per_kv)] for k in range(kv_heads)]
            block, other = lax.psum((block, other), "head", axis_index_groups=groups)
        block = block + swapped(other, "ctx", 0)
        for step in range(1, ctx_bits):
            pairs = [
                (c, c ^ (2**step if c % 2 == 0 else 2 ** (ctx_bits - step))) for c in range(ctx_count)
            ]
            block = block + lax.ppermute(block, "ctx", pairs)
        return block

    keys, values = spread(0), spread(1)

    def run(head_of, first, keys, values):
        return attend(head_of, first, keys, values, queries, row_mask, token_bias, kv_heads, images)

    def join(block):
        return block, swapped(block, "ctx", 0)

    if head_count != 4 or per_kv > 1:
        groups = [[k * per_kv + j for k in range(kv_heads)] for j in range(per_kv)]
        keys, values = (
            join(lax.all_gather(block, "head", axis_index_groups=groups))
            for block in (keys, values)
        )
        parts = []
        for k in range(kv_heads):
            halves = ([mine[k], other[k]] for mine, other in (keys, values))
            parts += run(lambda here, k=k: k, 0, *halves)
        return jnp.concatenate(parts, axis=1)

    held = [[], [], [], []]
    for block in (keys, values):

        def swap(value, pairs):
            return swap_middle(value) if pairs is MIDDLE else lax.ppermute(value, "head", pairs)

        near = swap(block, EDGES)
        inner = swap(block, MIDDLE)
        outer = swap(near, MIDDLE)
        inner = pick_by_place(inner, swap(inner, OUTWARD))
        outer = pick_by_place(outer, swap(outer, OUTWARD))
        for n, half in enumerate((block, near, inner, outer)):
            held[n].append(join(half))
    heads_of = [
        lambda here: here,
        lambda here: jnp.where(here % 2 == 0, here + 1, here - 1),
        lambda here: jnp.where(here < 2, 2, 1),
        lambda here: jnp.where(here < 2, 3, 0),
    ]
    parts = []
    for n in range(3):
        parts += run(heads_of[n], 0, *held[n])
    weighed = [run(heads_of[3], 0, held[3][0], None)]
    return mix_far(heads_of, held[3][1], weighed, row_mask, parts, images)


def solution(mesh):
    return jax.shard_map(
        shards,
        mesh=mesh,
        in_specs=(
            P(("ctx", "head"), None),
            P("ctx", "head"),
            P("head", None),
            P(),
            P("ctx", None),
            P(),
            P(),
        ),
        out_specs=P(("ctx", "head"), None),
        check_vma=False,
    )
```
